512 devices in a mesh: rows: 64 (over z, y), cols: 8 (over x, core).
Axes of the slice: x: 4, y: 8, z: 8, core: 2. Of those that a mesh axis runs over, the one named last changes fastest.
Arguments:
- momentum_codes: int32 [2, 8192, 8192], P(None, 'rows', 'cols'), may hold values from 0 to 255
- block_amax_scales: float32 [2, 8192, 4], P(None, 'rows'), may hold values from 0.05 to 1
- code_table: float32 [256], replicated, may hold values from -1 to 1
- gradient: bfloat16 [2, 8192, 8192], P(None, 'rows', 'cols'), may hold values from -4 to 4
- weight: bfloat16 [2, 8192, 8192], P(None, 'rows', 'cols'), may hold values from -6 to 6
- right_basis: bfloat16 [2, 8192, 256], P(None, 'cols'), may hold values from -0.0625 to 0.0625
Outputs:
- new_momentum: bfloat16 [2, 8192, 8192], P(None, 'rows', 'cols')
- fresh_block_scales: float32 [2, 8192, 4], P(None, 'rows')
- new_basis: bfloat16 [2, 8192, 256], P(None, 'cols')
- new_weight: bfloat16 [2, 8192, 8192], P(None, 'rows', 'cols')
The draws below stay inside these ranges and needn't reach their ends.
All inputs are finite; a program needn't handle non-finite values.
Results may differ from the reference program's by a relative error of at most 0.005.
Values sent between devices are 32-bit elements; how exact they have to be, the bound alone decides.
No kernel may reach another device: no remote copies, remote signals or barrier semaphores. Data moves between devices by JAX's collectives and lax.ppermute only.
A program may use at most 64 MiB of HBM per device.

```python
import math
import jax
import jax.numpy as jnp
from jax import lax

D = 8192
RANK = 256
BLOCK = 2048
LEVELS = 256
MATS = 2
NBLK = 4


def place_ends(drawn, rng, low, high):
    extent = drawn.shape
    index_at = [jax.random.randint(jax.random.fold_in(rng, axis), (), 0, extent[axis]) for axis in range(len(extent))]
    drawn = drawn.at[tuple(index_at)].set(low)
    longest = extent.index(max(extent))
    index_at[longest] = (index_at[longest] + 1) % extent[longest]
    return drawn.at[tuple(index_at)].set(high)


def shard_levels(key, shape, cuts, least, top_value):
    def one(axis_at, shards_of):
        heights = jax.random.uniform(jax.random.fold_in(jax.random.fold_in(key, 6), axis_at), (shards_of,), jnp.float32, least / len(cuts), top_value / len(cuts))
        return jnp.repeat(jnp.exp(heights), shape[axis_at] // shards_of).reshape((-1,) + (1,) * (len(shape) - axis_at - 1))

    factor_of = one(*cuts[0])
    for cut in cuts[1:]:
        factor_of = factor_of * one(*cut)
    return factor_of


def scatter_about(own_key, extent, spread, reach, pieces=(), held_as=jnp.bfloat16):
    values = jax.random.normal(own_key, extent, jnp.float32) * spread
    if len(pieces) > 0:
        values = shard_levels(own_key, extent, pieces, -0.22, 0.18) * values
    return jnp.clip(values, min=-reach, max=reach).astype(held_as)


def setup_inputs(seed: int = 0) -> dict:
    streams_of = jax.random.split(jax.random.key(seed), 7)
    return {
        "momentum_codes": place_ends(jax.random.randint(streams_of[0], (MATS, D, D), 0, LEVELS), jax.random.fold_in(streams_of[0], 1), 0, LEVELS - 1).astype(jnp.int32),
        "block_amax_scales": jnp.clip(jnp.exp(math.log(1.0) - 2.9957323 * jax.random.uniform(streams_of[1], (MATS, D, NBLK), jnp.float32) ** shard_levels(streams_of[1], (MATS, D, NBLK), ((1, 64),), -0.2, 0.2)), 0.05, 1.0),
        "code_table": jnp.clip(jax.random.uniform(streams_of[2], (LEVELS,), jnp.float32, -1.0, 1.0), -1.0, 1.0),
        "gradient": scatter_about(streams_of[3], (MATS, D, D), 0.5, 4.0, ((1, 64), (2, 8))),
        "weight": scatter_about(streams_of[4], (MATS, D, D), 1.0, 6.0, ((1, 64), (2, 8))),
        "right_basis": scatter_about(streams_of[5], (MATS, D, RANK), D ** -0.5, 0.0625, ((1, 8),)),
    }


epsilon = 1e-06
momentum_decay = 0.95
step_size = 0.5

def triangular_solved_rows(cholesky_lower, row_block):
    return jax.scipy.linalg.solve_triangular(cholesky_lower, row_block.T, lower=True).T

def reference(momentum_codes, block_amax_scales, code_table, gradient, weight, right_basis):
    peak_magnitude = lax.Precision.HIGHEST
    values = code_table[momentum_codes]
    scale_columns = jnp.repeat(block_amax_scales, BLOCK, axis=2)
    buffer = values * scale_columns + gradient.astype(jnp.float32)
    power_rows = jnp.einsum('mrn,mnk->mrk', buffer, right_basis.astype(jnp.float32), precision=peak_magnitude)
    basis_gram_product = jnp.einsum('mrk,mrl->mkl', power_rows, power_rows, precision=peak_magnitude)
    cholesky_lower = jnp.linalg.cholesky(basis_gram_product)
    ortho_rows = jax.vmap(triangular_solved_rows)(cholesky_lower, power_rows)
    back_rows = jnp.einsum('mrn,mrk->mnk', buffer, ortho_rows, precision=peak_magnitude)
    square_sums = lax.optimization_barrier(jnp.sum(back_rows * back_rows, axis=1))
    basis_full = back_rows * lax.rsqrt(square_sums + epsilon)[:, None, :]
    residual = buffer - (1.0 - momentum_decay) * jnp.einsum('mrk,mnk->mrn', ortho_rows, back_rows, precision=peak_magnitude)
    blocked = jnp.abs(residual).reshape(MATS, D, D // BLOCK, BLOCK)
    fresh_block_scales = lax.optimization_barrier(jnp.max(blocked, axis=3))
    new_momentum = (residual / (jnp.repeat(fresh_block_scales, BLOCK, axis=2) + epsilon)).astype(jnp.bfloat16)
    update = jnp.einsum('mrk,mnk->mrn', ortho_rows, basis_full, precision=peak_magnitude) * (D / math.sqrt(RANK))
    new_weight = (weight.astype(jnp.float32) - step_size * update).astype(jnp.bfloat16)
    return (new_momentum, fresh_block_scales, basis_full.astype(jnp.bfloat16), new_weight)
```

```python
import math

import jax
import jax.numpy as jnp
from jax import lax
from jax.experimental import pallas as pl
from jax.experimental.pallas import tpu as pltpu
from jax.sharding import Mesh
from jax.sharding import PartitionSpec as P

D = 8192
RANK = 256
BLOCK = 2048
LEVELS = 256
MATS = 2

epsilon = 1e-06
momentum_decay = 0.95
step_size = 0.5

ROWS = 128
COLS = 1024
HALF = COLS // 2
BLOCKED = 64
COLS_AXES = ("x", "core")
GROUP = ("yl", "x", "core")
OTHERS = ("zh", "zl", "yh")


def f32(*shape):
    return jax.ShapeDtypeStruct(shape, jnp.float32)


def high_dot(a, b, dims):
    return lax.dot_general(
        a, b, (dims, ((), ())), precision=lax.Precision.HIGHEST, preferred_element_type=jnp.float32
    )


def split_dot(a, b):
    total = None
    for _ in range(3):
        term = a.astype(jnp.bfloat16)
        a = a - term.astype(jnp.float32)
        part = jnp.dot(term, b, preferred_element_type=jnp.float32)
        total = part if total is None else total + part
    return total


def everyone(value, axes):
    count = lax.axis_size(axes)
    copies = jnp.broadcast_to(value, (count, *value.shape))
    return lax.all_to_all(copies, axes, 0, 0, tiled=True)


def decode_body(codes_ref, scale_ref, table_ref, grad_ref, basis_ref, halves_ref, power_ref):
    rows = codes_ref.shape[1]
    low = jnp.broadcast_to(table_ref[0:1], (rows, 128))
    high = jnp.broadcast_to(table_ref[1:2], (rows, 128))
    scale = scale_ref[0]
    pieces = []
    for t in range(COLS // 128):
        lanes = slice(t * 128, (t + 1) * 128)
        code = codes_ref[0, :, lanes]
        index = code & 127
        value = jnp.where(
            code < 128,
            jnp.take_along_axis(low, index, axis=1),
            jnp.take_along_axis(high, index, axis=1),
        )
        piece = value * scale + grad_ref[0, :, lanes].astype(jnp.float32)
        half, inner = divmod(t * 128, HALF)
        halves_ref[half, 0, :, inner : inner + 128] = piece
        pieces.append(piece)
    power_ref[0] = split_dot(jnp.concatenate(pieces, axis=1), basis_ref[0])


def decode(codes, scale, table, gradient, basis):
    tile = 64
    return pl.pallas_call(
        decode_body,
        grid=(MATS, ROWS // tile),
        in_specs=[
            pl.BlockSpec((1, tile, COLS), lambda m, i: (m, i, 0)),
            pl.BlockSpec((1, tile, 1), lambda m, i: (m, i, 0)),
            pl.BlockSpec((2, 128), lambda m, i: (0, 0)),
            pl.BlockSpec((1, tile, COLS), lambda m, i: (m, i, 0)),
            pl.BlockSpec((1, COLS, RANK), lambda m, i: (m, 0, 0)),
        ],
        out_specs=[
            pl.BlockSpec((2, 1, tile, HALF), lambda m, i: (0, m, i, 0)),
            pl.BlockSpec((1, tile, RANK), lambda m, i: (m, i, 0)),
        ],
        out_shape=[f32(2, MATS, ROWS, HALF), f32(MATS, ROWS, RANK)],
        cost_estimate=pl.CostEstimate(flops=400_000_000, bytes_accessed=4_000_000, transcendentals=0),
        name="decode",
    )(codes, scale, table, gradient, basis)


def gram_body(slot_ref, power_ref, gram_ref, whole_ref):
    for m in range(MATS):
        rows = jnp.concatenate([power_ref[0, m], power_ref[1, m]], axis=0)
        whole_ref[m * RANK : (m + 1) * RANK] = high_dot(rows, rows, ((0,), (0,)))
    gram_ref[...] = whole_ref[pl.ds(pl.multiple_of(slot_ref[0] * 32, 32), 32), :]


def gram_slice(slot, power):
    return pl.pallas_call(
        gram_body,
        in_specs=[
            pl.BlockSpec(memory_space=pltpu.SMEM),
            pl.BlockSpec(memory_space=pltpu.VMEM),
        ],
        out_specs=pl.BlockSpec(memory_space=pltpu.VMEM),
        out_shape=f32(32, RANK),
        scratch_shapes=[pltpu.VMEM((MATS * RANK, RANK), jnp.float32)],
        cost_estimate=pl.CostEstimate(flops=400_000_000, bytes_accessed=600_000, transcendentals=0),
        name="gram_slice",
    )(slot, power)


def cross_body(buffer_ref, power_ref, cross_ref):
    for m in range(MATS):
        left = jnp.concatenate([buffer_ref[0, m], buffer_ref[1, m]], axis=0)
        right = jnp.concatenate([power_ref[0, m], power_ref[1, m]], axis=0)
        cross_ref[m] = high_dot(left, right, ((0,), (0,)))


def cross(buffer, power):
    return pl.pallas_call(
        cross_body,
        in_specs=[pl.BlockSpec(memory_space=pltpu.VMEM)] * 2,
        out_specs=pl.BlockSpec(memory_space=pltpu.VMEM),
        out_shape=f32(MATS, HALF, RANK),
        cost_estimate=pl.CostEstimate(flops=800_000_000, bytes_accessed=2_600_000, transcendentals=0),
        name="cross",
    )(buffer, power)


def eliminate(block):
    n = BLOCKED
    tiles = [block[8 * t : 8 * t + 8] for t in range(n // 8)]
    sub = lax.broadcasted_iota(jnp.int32, (8, 2 * n), 0)
    done = []
    for j in range(0, n, 2):
        t, s = divmod(j, 8)
        row1 = tiles[t][s : s + 1]
        row2 = tiles[t][s + 1 : s + 2]
        a = row1[:, j : j + 1]
        b = row1[:, j + 1 : j + 2]
        c = row2[:, j + 1 : j + 2]
        det = a * c - b * b
        inv_det = 1.0 / det
        step1 = (c * inv_det) * row1 - (b * inv_det) * row2
        step2 = (a * inv_det) * row2 - (b * inv_det) * row1
        done += [row1 * lax.rsqrt(a), (row2 - (b / a) * row1) * lax.rsqrt(det / a)]
        for u in range(t, n // 8):
            if u == t and s == 6:
                continue
            change = tiles[u][:, j : j + 1] * step1 + tiles[u][:, j + 1 : j + 2] * step2
            if u == t:
                change = jnp.where(sub > s + 1, change, 0.0)
            tiles[u] = tiles[u] - change
    return jnp.concatenate(done, axis=0)


def factor_body(gram_ref, inv_ref, schur_ref):
    n = BLOCKED
    row = lax.broadcasted_iota(jnp.int32, (RANK, RANK), 0)
    col = lax.broadcasted_iota(jnp.int32, (RANK, RANK), 1)
    identity = (row == col).astype(jnp.float32)
    for m in range(MATS):
        schur_ref[m] = gram_ref[m]
        inv_ref[m] = identity
    lane = lax.broadcasted_iota(jnp.int32, (n, 2 * n), 1)
    sub = lax.broadcasted_iota(jnp.int32, (n, 2 * n), 0)
    eye = (lane == sub + n).astype(jnp.float32)
    col_id = lax.broadcasted_iota(jnp.int32, (n, RANK), 1)

    def one_block(k, carry):
        at = pl.multiple_of(k * n, n)
        blocks = []
        for m in range(MATS):
            rows = schur_ref[m, pl.ds(at, n), :]
            turned = pltpu.roll(rows, lax.rem(RANK - at, RANK), 1)
            blocks.append(jnp.where(lane < n, turned[:, : 2 * n], eye))
        both = [eliminate(block) for block in blocks]
        for m in range(MATS):
            low_inv = pltpu.roll(both[m], n, 1)[:, :n]
            upper = high_dot(low_inv, schur_ref[m, pl.ds(at, n), :], ((1,), (0,)))
            fresh = high_dot(low_inv, inv_ref[m, pl.ds(at, n), :], ((1,), (0,)))
            upper = jnp.where(col_id >= at + n, upper, 0.0)
            schur_ref[m] = schur_ref[m] - high_dot(upper, upper, ((0,), (0,)))
            inv_ref[m] = inv_ref[m] - high_dot(upper, fresh, ((0,), (0,)))
            inv_ref[m, pl.ds(at, n), :] = fresh
        return carry

    lax.fori_loop(0, RANK // n, one_block, 0)


def inverse_factor(gram):
    return pl.pallas_call(
        factor_body,
        in_specs=[pl.BlockSpec(memory_space=pltpu.VMEM)],
        out_specs=pl.BlockSpec(memory_space=pltpu.VMEM),
        out_shape=f32(MATS, RANK, RANK),
        scratch_shapes=[pltpu.VMEM((MATS, RANK, RANK), jnp.float32)],
        cost_estimate=pl.CostEstimate(
            flops=20_000_000_000, bytes_accessed=1_000_000, transcendentals=0
        ),
        name="inverse_factor",
    )(gram)


def turned_row(column):
    return jnp.transpose(jnp.broadcast_to(column, (ROWS, 128)))[0:1]


def finish_body(
    place_ref, inv_ref, power_ref, own_ref, other_ref, halves_ref,
    back_ref, ortho_ref, residual_ref, small_ref,
):
    place = place_ref[0]
    small = []
    peaks = []
    for m in range(MATS):
        factor = inv_ref[m]
        own = high_dot(own_ref[m], factor, ((1,), (1,)))
        other = high_dot(other_ref[m], factor, ((1,), (1,)))
        back_ref[m, pl.ds(pl.multiple_of(place * HALF, HALF), HALF), :] = own
        back_ref[m, pl.ds(pl.multiple_of((1 - place) * HALF, HALF), HALF), :] = other
        small.append(
            jnp.sum(own * own, axis=0, keepdims=True) + jnp.sum(other * other, axis=0, keepdims=True)
        )
        ortho = high_dot(power_ref[m], factor, ((1,), (1,)))
        ortho_ref[m] = ortho
        peak = None
        for h in range(2):
            back = back_ref[m, h * HALF : (h + 1) * HALF, :]
            residual = halves_ref[h, m] - (1.0 - momentum_decay) * high_dot(
                ortho, back, ((1,), (1,))
            )
            residual_ref[m, :, h * HALF : (h + 1) * HALF] = residual
            top = jnp.max(jnp.abs(residual), axis=1, keepdims=True)
            peak = top if peak is None else jnp.maximum(peak, top)
        peaks.append(turned_row(peak))
    for m in range(MATS):
        small_ref[2 * m : 2 * m + 1] = small[m][:, :128]
        small_ref[2 * m + 1 : 2 * m + 2] = small[m][:, 128:]
        small_ref[4 + m : 5 + m] = peaks[m]
    small_ref[6:8] = jnp.zeros((2, 128), jnp.float32)


def finish(place, inv, power, own, other, halves):
    return pl.pallas_call(
        finish_body,
        in_specs=[pl.BlockSpec(memory_space=pltpu.SMEM)]
        + [pl.BlockSpec(memory_space=pltpu.VMEM)] * 5,
        out_specs=[pl.BlockSpec(memory_space=pltpu.VMEM)] * 4,
        out_shape=[
            f32(MATS, COLS, RANK),
            f32(MATS, ROWS, RANK),
            f32(MATS, ROWS, COLS),
            f32(8, 128),
        ],
        cost_estimate=pl.CostEstimate(
            flops=2_500_000_000, bytes_accessed=7_000_000, transcendentals=0
        ),
        name="finish",
    )(place, inv, power, own, other, halves)


def turned_column(row):
    return jnp.transpose(jnp.broadcast_to(row, (128, ROWS)))


def outputs_body(
    block_ref, small_ref, back_ref, ortho_ref, residual_ref, weight_ref,
    momentum_ref, peaks_ref, basis_ref, new_weight_ref,
):
    total = small_ref[0]
    for i in range(1, 8):
        total = total + small_ref[i]
    block = block_ref[0]
    for m in range(MATS):
        squares = jnp.concatenate([total[2 * m : 2 * m + 1], total[2 * m + 1 : 2 * m + 2]], axis=1)
        norm = lax.rsqrt(squares + epsilon)
        basis = back_ref[m] * norm
        basis_ref[m] = basis.astype(jnp.bfloat16)
        peaks = [
            jnp.maximum(small_ref[2 * b, 4 + m : 5 + m], small_ref[2 * b + 1, 4 + m : 5 + m])
            for b in range(D // BLOCK)
        ]
        for b in range(D // BLOCK):
            peaks_ref[m, b : b + 1] = peaks[b]
        mine = jnp.maximum(
            small_ref[2 * block, 4 + m : 5 + m], small_ref[2 * block + 1, 4 + m : 5 + m]
        )
        scale = turned_column(mine) + epsilon
        scale = jnp.concatenate([scale] * (COLS // 128), axis=1)
        momentum_ref[m] = (residual_ref[m] / scale).astype(jnp.bfloat16)
        update = high_dot(ortho_ref[m], basis, ((1,), (1,))) * (D / math.sqrt(RANK))
        new_weight_ref[m] = (weight_ref[m].astype(jnp.float32) - step_size * update).astype(
            jnp.bfloat16
        )


def outputs(block, small, back, ortho, residual, weight):
    return pl.pallas_call(
        outputs_body,
        in_specs=[pl.BlockSpec(memory_space=pltpu.SMEM)]
        + [pl.BlockSpec(memory_space=pltpu.VMEM)] * 5,
        out_specs=[pl.BlockSpec(memory_space=pltpu.VMEM)] * 4,
        out_shape=[
            jax.ShapeDtypeStruct((MATS, ROWS, COLS), jnp.bfloat16),
            f32(MATS, D // BLOCK, ROWS),
            jax.ShapeDtypeStruct((MATS, COLS, RANK), jnp.bfloat16),
            jax.ShapeDtypeStruct((MATS, ROWS, COLS), jnp.bfloat16),
        ],
        cost_estimate=pl.CostEstimate(
            flops=900_000_000, bytes_accessed=7_000_000, transcendentals=0
        ),
        name="outputs",
    )(block, small, back, ortho, residual, weight)


def row_shift(step):
    return [(i, i // 8 * 8 + (i + step) % 8) for i in range(64)]


def per_device(codes, scales, table, gradient, weight, basis):
    place = lax.axis_index("yl")
    block = lax.axis_index("x")
    slot = lax.axis_index(GROUP)
    scale = lax.dynamic_slice_in_dim(scales, block, 1, axis=2)
    halves, partial_power = decode(codes, scale, table.reshape(2, 128), gradient, basis)

    with jax.named_scope("swap"):
        buffer = lax.all_to_all(halves, "yl", 0, 0, tiled=True)

    with jax.named_scope("power_sum"):
        pieces = lax.all_to_all(
            partial_power.reshape(8, 32, RANK), COLS_AXES, 0, 0, tiled=True
        )
        piece = jnp.sum(pieces, axis=0)
    with jax.named_scope("power_all"):
        power = everyone(piece, GROUP).reshape(2, MATS, ROWS, RANK)
    own_power = lax.dynamic_index_in_dim(power, place, 0, keepdims=False)

    partial_cross = cross(buffer, power)
    with jax.named_scope("cross_sum"):
        pieces = lax.all_to_all(partial_cross.reshape(32, 32, RANK), OTHERS, 0, 0, tiled=True)

    gram = gram_slice(slot.astype(jnp.int32).reshape(1), power)
    with jax.named_scope("gram_z"):
        gram = jnp.sum(everyone(gram, ("zh", "zl")), axis=0)
    with jax.named_scope("gram_y"):
        gram = jnp.sum(everyone(gram, "yh"), axis=0)
    with jax.named_scope("gram_all"):
        gram = everyone(gram, GROUP).reshape(MATS, RANK, RANK)

    cross_piece = jnp.sum(pieces, axis=0)
    with jax.named_scope("cross_all"):
        own = everyone(cross_piece, OTHERS).reshape(MATS, HALF, RANK)
    inv = inverse_factor(gram)
    with jax.named_scope("cross_pair"):
        rows_axes = ("zh", "zl", "yh", "yl")
        first = lax.ppermute(own[0], rows_axes, row_shift(1))
        second = lax.ppermute(own[1], rows_axes, row_shift(7))
        other = jnp.stack([first, second])

    back, ortho, residual, small = finish(
        place.astype(jnp.int32).reshape(1), inv, own_power, own, other, halves
    )
    with jax.named_scope("small"):
        small = everyone(small, COLS_AXES)
    new_momentum, peaks, new_basis, new_weight = outputs(
        block.astype(jnp.int32).reshape(1), small, back, ortho, residual, weight
    )
    return new_momentum, jnp.swapaxes(peaks, 1, 2), new_basis, new_weight


def solution(mesh):
    axes = ("zh", "zl", "yh", "yl", "x", "core")
    fine = Mesh(mesh.devices.reshape(4, 2, 4, 2, 4, 2), axes)
    rows = axes[:4]
    cols = axes[4:]
    return jax.shard_map(
        per_device,
        mesh=fine,
        in_specs=(
            P(None, rows, cols),
            P(None, rows, None),
            P(),
            P(None, rows, cols),
            P(None, rows, cols),
            P(None, cols, None),
        ),
        out_specs=(
            P(None, rows, cols),
            P(None, rows, None),
            P(None, cols, None),
            P(None, rows, cols),
        ),
        check_vma=False,
    )
```

```python
import math

import jax
import jax.numpy as jnp
from jax import lax
from jax.experimental import pallas as pl
from jax.experimental.pallas import tpu as pltpu
from jax.sharding import Mesh
from jax.sharding import PartitionSpec as P


D = 8192
RANK = 256
BLOCK = 2048
MATS = 2

epsilon = 1e-06
momentum_decay = 0.95
step_size = 0.5

ROWS = 128
COLS = 1024
HALF = COLS // 2
BLOCKED = 64
COLS_AXES = ("x", "core")
GROUP = ("yl", "x", "core")
OTHERS = ("zh", "zl", "yh")


def f32(*shape):
    return jax.ShapeDtypeStruct(shape, jnp.float32)


def high_dot(a, b, dims):
    return lax.dot_general(
        a, b, (dims, ((), ())), precision=lax.Precision.HIGHEST, preferred_element_type=jnp.float32
    )


def split_dot(a, b):
    total = None
    for _ in range(3):
        term = a.astype(jnp.bfloat16)
        a = a - term.astype(jnp.float32)
        part = jnp.dot(term, b, preferred_element_type=jnp.float32)
        total = part if total is None else total + part
    return total


def everyone(value, axes):
    count = lax.axis_size(axes)
    copies = jnp.broadcast_to(value, (count, *value.shape))
    return lax.all_to_all(copies, axes, 0, 0, tiled=True)


def decode_body(place_ref, codes_ref, scale_ref, table_ref, grad_ref, basis_ref, halves_ref, power_ref):
    rows = codes_ref.shape[1]
    low = jnp.broadcast_to(table_ref[0:1], (rows, 128))
    high = jnp.broadcast_to(table_ref[1:2], (rows, 128))
    scale = scale_ref[0]
    pieces = []
    for t in range(COLS // 128):
        lanes = slice(t * 128, (t + 1) * 128)
        code = codes_ref[0, :, lanes]
        index = code & 127
        value = jnp.where(
            code < 128,
            jnp.take_along_axis(low, index, axis=1),
            jnp.take_along_axis(high, index, axis=1),
        )
        piece = value * scale + grad_ref[0, :, lanes].astype(jnp.float32)
        half, inner = divmod(t * 128, HALF)
        halves_ref[(half + place_ref[0]) % 2, 0, :, inner : inner + 128] = piece
        pieces.append(piece)
    power_ref[0] = split_dot(jnp.concatenate(pieces, axis=1), basis_ref[0])


def decode(place, codes, scale, table, gradient, basis):
    tile = 64
    return pl.pallas_call(
        decode_body,
        grid=(MATS, ROWS // tile),
        in_specs=[
            pl.BlockSpec(memory_space=pltpu.SMEM),
            pl.BlockSpec((1, tile, COLS), lambda m, i: (m, i, 0)),
            pl.BlockSpec((1, tile, 1), lambda m, i: (m, i, 0)),
            pl.BlockSpec((2, 128), lambda m, i: (0, 0)),
            pl.BlockSpec((1, tile, COLS), lambda m, i: (m, i, 0)),
            pl.BlockSpec((1, COLS, RANK), lambda m, i: (m, 0, 0)),
        ],
        out_specs=[
            pl.BlockSpec((2, 1, tile, HALF), lambda m, i: (0, m, i, 0)),
            pl.BlockSpec((1, tile, RANK), lambda m, i: (m, i, 0)),
        ],
        out_shape=[f32(2, MATS, ROWS, HALF), f32(MATS, ROWS, RANK)],
        cost_estimate=pl.CostEstimate(flops=400_000_000, bytes_accessed=4_000_000, transcendentals=0),
        name="decode",
    )(place, codes, scale, table, gradient, basis)


def gram_body(slot_ref, power_ref, gram_ref, whole_ref):
    for m in range(MATS):
        rows = jnp.concatenate([power_ref[0, m], power_ref[1, m]], axis=0)
        whole_ref[m * RANK : (m + 1) * RANK] = high_dot(rows, rows, ((0,), (0,)))
    gram_ref[...] = whole_ref[pl.ds(pl.multiple_of(slot_ref[0] * 32, 32), 32), :]


def gram_slice(slot, power):
    return pl.pallas_call(
        gram_body,
        in_specs=[
            pl.BlockSpec(memory_space=pltpu.SMEM),
            pl.BlockSpec(memory_space=pltpu.VMEM),
        ],
        out_specs=pl.BlockSpec(memory_space=pltpu.VMEM),
        out_shape=f32(32, RANK),
        scratch_shapes=[pltpu.VMEM((MATS * RANK, RANK), jnp.float32)],
        cost_estimate=pl.CostEstimate(flops=400_000_000, bytes_accessed=600_000, transcendentals=0),
        name="gram_slice",
    )(slot, power)


def cross_body(place_ref, halves_ref, received_ref, power_ref, cross_ref):
    place = place_ref[0]
    for m in range(MATS):
        left = jnp.concatenate([halves_ref[0, m], received_ref[m]], axis=0)
        right = jnp.concatenate([power_ref[place, m], power_ref[1 - place, m]], axis=0)
        cross_ref[m] = high_dot(left, right, ((0,), (0,)))


def cross(place, halves, received, power):
    return pl.pallas_call(
        cross_body,
        in_specs=[pl.BlockSpec(memory_space=pltpu.SMEM)]
        + [pl.BlockSpec(memory_space=pltpu.VMEM)] * 3,
        out_specs=pl.BlockSpec(memory_space=pltpu.VMEM),
        out_shape=f32(MATS, HALF, RANK),
        cost_estimate=pl.CostEstimate(flops=800_000_000, bytes_accessed=2_600_000, transcendentals=0),
        name="cross",
    )(place, halves, received, power)


def lane_copy(tile, lane):
    return jnp.broadcast_to(tile[:, lane : lane + 1], (8, 128))


def row_copy(tile, row):
    return jnp.broadcast_to(tile[row : row + 1], (8, 128))


def eliminate(tiles, base):
    sub = lax.broadcasted_iota(jnp.int32, (8, 128), 0)
    tiles = list(tiles)
    done = []
    for t in range(8):
        at = base + 8 * t
        work = [lane_copy(tiles[t], at + i) for i in range(8)] + [tiles[t]]
        steps = []
        rows = [None] * 8
        for p in range(0, 8, 2):
            a = row_copy(work[p], p)
            b = row_copy(work[p + 1], p)
            c = row_copy(work[p + 1], p + 1)
            det = a * c - b * b
            inv_det = 1.0 / det
            ca, cb, cc = a * inv_det, b * inv_det, c * inv_det
            later = sub > p + 1
            left = jnp.where(later, work[p], 0.0)
            right = jnp.where(later, work[p + 1], 0.0)
            step = {}
            for i in range(p + 2, 9):
                x = row_copy(work[i], p)
                y = row_copy(work[i], p + 1)
                step[i] = (cc * x - cb * y, ca * y - cb * x)
                if i == 8:
                    rows[p] = x * lax.rsqrt(a)
                    rows[p + 1] = (y - (b / a) * x) * lax.rsqrt(det / a)
                work[i] = work[i] - (left * step[i][0] + right * step[i][1])
            steps.append(step)
        out = rows[0]
        for p in range(1, 8):
            out = jnp.where(sub == p, rows[p], out)
        done.append(out)
        for u in range(t + 1, 8):
            work = [lane_copy(tiles[u], at + i) for i in range(8)] + [tiles[u]]
            for p in range(0, 8, 2):
                step = steps[p // 2]
                for i in range(p + 2, 9):
                    work[i] = work[i] - (work[p] * step[i][0] + work[p + 1] * step[i][1])
            tiles[u] = work[8]
    return jnp.concatenate(done, axis=0)


def factor_body(gram_ref, inv_ref, state_ref):
    n = BLOCKED
    lane = lax.broadcasted_iota(jnp.int32, (n, 128), 1)
    sub = lax.broadcasted_iota(jnp.int32, (n, 128), 0)
    wide = lax.broadcasted_iota(jnp.int32, (n, RANK), 1)
    deep = lax.broadcasted_iota(jnp.int32, (n, RANK), 0)
    for m in range(MATS):
        state_ref[m] = gram_ref[m]
    for k in range(RANK // n):
        at = k * n
        base = at % 128
        mine = (lane >= base) & (lane < base + n)
        eye = (jnp.where(lane < n, lane, lane - n) == sub).astype(jnp.float32)
        reduced = []
        for m in range(MATS):
            pair = state_ref[m, at : at + n, at - base : at - base + 128]
            block = jnp.where(mine, pair, eye)
            reduced.append(eliminate([block[8 * t : 8 * t + 8] for t in range(8)], base))
        for m in range(MATS):
            low_inv = jnp.where(mine, 0.0, reduced[m])
            rows = jnp.where(
                (wide >= at) & (wide < at + n),
                (wide - at == deep).astype(jnp.float32),
                state_ref[m, at : at + n, :],
            )
            fresh = high_dot(low_inv, jnp.concatenate([rows, rows], axis=0), ((1,), (0,)))
            inv_ref[m, at : at + n, :] = jnp.where(wide < at + n, fresh, 0.0)
            if k == RANK // n - 1:
                continue
            start = (at + n) // 128 * 128
            upper = jnp.where(wide >= at + n, fresh, 0.0)[:, start:]
            change = high_dot(upper, fresh, ((0,), (0,)))
            for r in range(at + n, RANK, n):
                old = state_ref[m, r : r + n, :]
                old = jnp.where((wide >= at) & (wide < at + n), 0.0, old)
                state_ref[m, r : r + n, :] = old - change[r - start : r - start + n]


def inverse_factor(gram):
    return pl.pallas_call(
        factor_body,
        in_specs=[pl.BlockSpec(memory_space=pltpu.VMEM)],
        out_specs=pl.BlockSpec(memory_space=pltpu.VMEM),
        out_shape=f32(MATS, RANK, RANK),
        scratch_shapes=[pltpu.VMEM((MATS, RANK, RANK), jnp.float32)],
        cost_estimate=pl.CostEstimate(
            flops=4_000_000_000, bytes_accessed=1_000_000, transcendentals=0
        ),
        name="inverse_factor",
    )(gram)


def turned_row(column):
    return jnp.transpose(jnp.broadcast_to(column, (ROWS, 128)))[0:1]


def finish_body(
    place_ref, inv_ref, power_ref, own_ref, first_ref, second_ref, halves_ref,
    back_ref, ortho_ref, residual_ref, small_ref,
):
    place = place_ref[0]
    small = []
    peaks = []
    for m in range(MATS):
        factor = inv_ref[m]
        ortho = high_dot(power_ref[place, m], factor, ((1,), (1,)))
        ortho_ref[m] = ortho
        squares = None
        peak = None
        for h in range(2):
            summed = own_ref[m] if h == 0 else (first_ref, second_ref)[m][...]
            back = high_dot(summed, factor, ((1,), (1,)))
            at = pl.ds(pl.multiple_of((place + h) % 2 * HALF, HALF), HALF)
            back_ref[m, at, :] = back
            part = jnp.sum(back * back, axis=0, keepdims=True)
            squares = part if squares is None else squares + part
            residual = halves_ref[h, m] - (1.0 - momentum_decay) * high_dot(
                ortho, back, ((1,), (1,))
            )
            residual_ref[m, :, at] = residual
            top = jnp.max(jnp.abs(residual), axis=1, keepdims=True)
            peak = top if peak is None else jnp.maximum(peak, top)
        small.append(squares)
        peaks.append(turned_row(peak))
    for m in range(MATS):
        small_ref[2 * m : 2 * m + 1] = small[m][:, :128]
        small_ref[2 * m + 1 : 2 * m + 2] = small[m][:, 128:]
        small_ref[4 + m : 5 + m] = peaks[m]
    small_ref[6:8] = jnp.zeros((2, 128), jnp.float32)


def finish(place, inv, power, own, first, second, halves):
    return pl.pallas_call(
        finish_body,
        in_specs=[pl.BlockSpec(memory_space=pltpu.SMEM)]
        + [pl.BlockSpec(memory_space=pltpu.VMEM)] * 6,
        out_specs=[pl.BlockSpec(memory_space=pltpu.VMEM)] * 4,
        out_shape=[
            f32(MATS, COLS, RANK),
            f32(MATS, ROWS, RANK),
            f32(MATS, ROWS, COLS),
            f32(8, 128),
        ],
        cost_estimate=pl.CostEstimate(
            flops=2_500_000_000, bytes_accessed=7_000_000, transcendentals=0
        ),
        name="finish",
    )(place, inv, power, own, first, second, halves)


def turned_column(row):
    return jnp.transpose(jnp.broadcast_to(row, (128, ROWS)))


def outputs_body(
    block_ref, small_ref, back_ref, ortho_ref, residual_ref, weight_ref,
    momentum_ref, peaks_ref, basis_ref, new_weight_ref,
):
    total = small_ref[0]
    for i in range(1, 8):
        total = total + small_ref[i]
    block = block_ref[0]
    for m in range(MATS):
        squares = jnp.concatenate([total[2 * m : 2 * m + 1], total[2 * m + 1 : 2 * m + 2]], axis=1)
        norm = lax.rsqrt(squares + epsilon)
        basis = back_ref[m] * norm
        basis_ref[m] = basis.astype(jnp.bfloat16)
        peaks = [
            jnp.maximum(small_ref[2 * b, 4 + m : 5 + m], small_ref[2 * b + 1, 4 + m : 5 + m])
            for b in range(D // BLOCK)
        ]
        for b in range(D // BLOCK):
            peaks_ref[m, b : b + 1] = peaks[b]
        mine = jnp.maximum(
            small_ref[2 * block, 4 + m : 5 + m], small_ref[2 * block + 1, 4 + m : 5 + m]
        )
        scale = turned_column(mine) + epsilon
        scale = jnp.concatenate([scale] * (COLS // 128), axis=1)
        momentum_ref[m] = (residual_ref[m] / scale).astype(jnp.bfloat16)
        update = high_dot(ortho_ref[m], basis, ((1,), (1,))) * (D / math.sqrt(RANK))
        new_weight_ref[m] = (weight_ref[m].astype(jnp.float32) - step_size * update).astype(
            jnp.bfloat16
        )


def outputs(block, small, back, ortho, residual, weight):
    return pl.pallas_call(
        outputs_body,
        in_specs=[pl.BlockSpec(memory_space=pltpu.SMEM)]
        + [pl.BlockSpec(memory_space=pltpu.VMEM)] * 5,
        out_specs=[pl.BlockSpec(memory_space=pltpu.VMEM)] * 4,
        out_shape=[
            jax.ShapeDtypeStruct((MATS, ROWS, COLS), jnp.bfloat16),
            f32(MATS, D // BLOCK, ROWS),
            jax.ShapeDtypeStruct((MATS, COLS, RANK), jnp.bfloat16),
            jax.ShapeDtypeStruct((MATS, ROWS, COLS), jnp.bfloat16),
        ],
        cost_estimate=pl.CostEstimate(
            flops=900_000_000, bytes_accessed=7_000_000, transcendentals=0
        ),
        name="outputs",
    )(block, small, back, ortho, residual, weight)


def row_shift(step):
    return [(i, i // 8 * 8 + (i + step) % 8) for i in range(64)]


def per_device(codes, scales, table, gradient, weight, basis):
    place = lax.axis_index("yl").astype(jnp.int32).reshape(1)
    block = lax.axis_index("x").astype(jnp.int32)
    slot = lax.axis_index(GROUP).astype(jnp.int32).reshape(1)
    scale = lax.dynamic_slice_in_dim(scales, block, 1, axis=2)
    halves, partial_power = decode(place, codes, scale, table.reshape(2, 128), gradient, basis)

    received = lax.ppermute(halves[1], "yl", [(0, 1), (1, 0)])

    pieces = lax.all_to_all(partial_power.reshape(8, 32, RANK), COLS_AXES, 0, 0, tiled=True)
    piece = jnp.sum(pieces, axis=0)
    power = everyone(piece, GROUP).reshape(2, MATS, ROWS, RANK)

    partial_cross = cross(place, halves, received, power)
    pieces = lax.all_to_all(partial_cross.reshape(32, 32, RANK), OTHERS, 0, 0, tiled=True)

    gram = gram_slice(slot, power)
    gram = jnp.sum(lax.all_gather(gram, ("zh", "zl")), axis=0)
    gram = jnp.sum(lax.all_gather(gram, "yh"), axis=0)
    gram = lax.all_gather(gram, GROUP).reshape(MATS, RANK, RANK)

    cross_piece = jnp.sum(pieces, axis=0)
    own = everyone(cross_piece, OTHERS).reshape(MATS, HALF, RANK)
    inv = inverse_factor(gram)
    rows_axes = ("zh", "zl", "yh", "yl")
    first = lax.ppermute(own[0], rows_axes, row_shift(1))
    second = lax.ppermute(own[1], rows_axes, row_shift(7))

    back, ortho, residual, small = finish(place, inv, power, own, first, second, halves)
    small = everyone(small, COLS_AXES)
    new_momentum, peaks, new_basis, new_weight = outputs(
        block.reshape(1), small, back, ortho, residual, weight
    )
    return new_momentum, jnp.swapaxes(peaks, 1, 2), new_basis, new_weight


def solution(mesh):
    axes = ("zh", "zl", "yh", "yl", "x", "core")
    fine = Mesh(mesh.devices.reshape(4, 2, 4, 2, 4, 2), axes)
    rows = axes[:4]
    cols = axes[4:]
    return jax.shard_map(
        per_device,
        mesh=fine,
        in_specs=(
            P(None, rows, cols),
            P(None, rows, None),
            P(),
            P(None, rows, cols),
            P(None, rows, cols),
            P(None, cols, None),
        ),
        out_specs=(
            P(None, rows, cols),
            P(None, rows, None),
            P(None, cols, None),
            P(None, rows, cols),
        ),
        check_vma=False,
    )
```

```python
import math

import jax
import jax.numpy as jnp
from jax import lax
from jax.experimental import pallas as pl
from jax.experimental.pallas import tpu as pltpu
from jax.sharding import Mesh
from jax.sharding import PartitionSpec as P


D = 8192
RANK = 256
BLOCK = 2048
MATS = 2

epsilon = 1e-06
momentum_decay = 0.95
step_size = 0.5

ROWS = 128
COLS = 1024
HALF = COLS // 2
PIECE = 72
BLOCKED = 64
COLS_AXES = ("x", "core")
GROUP = ("yl", "x", "core")
OTHERS = ("zh", "zl", "yh")


def f32(*shape):
    return jax.ShapeDtypeStruct(shape, jnp.float32)


def high_dot(a, b, dims):
    return lax.dot_general(
        a, b, (dims, ((), ())), precision=lax.Precision.HIGHEST, preferred_element_type=jnp.float32
    )


def split_dot(a, b):
    total = None
    for _ in range(3):
        term = a.astype(jnp.bfloat16)
        a = a - term.astype(jnp.float32)
        part = jnp.dot(term, b, preferred_element_type=jnp.float32)
        total = part if total is None else total + part
    return total


def near_dot(a, b, dims):
    a_top = a.astype(jnp.bfloat16)
    b_top = b.astype(jnp.bfloat16)
    a_rest = (a - a_top.astype(jnp.float32)).astype(jnp.bfloat16)
    b_rest = (b - b_top.astype(jnp.float32)).astype(jnp.bfloat16)

    def dot(x, y):
        return lax.dot_general(x, y, (dims, ((), ())), preferred_element_type=jnp.float32)

    return dot(a_top, b_top) + (dot(a_top, b_rest) + dot(a_rest, b_top))


def params():
    return pltpu.CompilerParams(vmem_limit_bytes=24 * 1024 * 1024)


def everyone(value, axes):
    count = lax.axis_size(axes)
    copies = jnp.broadcast_to(value, (count, *value.shape))
    return lax.all_to_all(copies, axes, 0, 0, tiled=True)


def turned_row(column):
    return jnp.transpose(jnp.broadcast_to(column, (ROWS, 128)))[0:1]


def turned_column(row):
    return jnp.transpose(jnp.broadcast_to(row, (128, ROWS)))


def decode_body(
    place_ref, codes_ref, scale_ref, table_ref, grad_ref, basis_ref, kept_ref, sent_ref, power_ref
):
    place, block = place_ref[0], place_ref[1]
    low = jnp.broadcast_to(table_ref[0:1], (ROWS, 128))
    high = jnp.broadcast_to(table_ref[1:2], (ROWS, 128))
    scale = turned_column(scale_ref[0, pl.ds(block, 1), :])
    power = None
    for half, out_ref in ((place, kept_ref), (1 - place, sent_ref)):
        pieces = []
        for t in range(HALF // 128):
            lanes = pl.ds(pl.multiple_of(half * HALF + t * 128, 128), 128)
            code = codes_ref[0, :, lanes]
            index = code & 127
            value = jnp.where(
                code < 128,
                jnp.take_along_axis(low, index, axis=1),
                jnp.take_along_axis(high, index, axis=1),
            )
            pieces.append(value * scale + grad_ref[0, :, lanes].astype(jnp.float32))
        piece = jnp.concatenate(pieces, axis=1)
        out_ref[0] = piece
        part = split_dot(piece, basis_ref[0, pl.ds(pl.multiple_of(half * HALF, HALF), HALF), :])
        power = part if power is None else power + part
    power_ref[0] = power


def decode(place, codes, scales, table, gradient, basis):
    return pl.pallas_call(
        decode_body,
        grid=(MATS,),
        in_specs=[
            pl.BlockSpec(memory_space=pltpu.SMEM),
            pl.BlockSpec((1, ROWS, COLS), lambda m: (m, 0, 0)),
            pl.BlockSpec((1, D // BLOCK, ROWS), lambda m: (m, 0, 0)),
            pl.BlockSpec((2, 128), lambda m: (0, 0)),
            pl.BlockSpec((1, ROWS, COLS), lambda m: (m, 0, 0)),
            pl.BlockSpec((1, COLS, RANK), lambda m: (m, 0, 0)),
        ],
        out_specs=[
            pl.BlockSpec((1, ROWS, HALF), lambda m: (m, 0, 0)),
            pl.BlockSpec((1, ROWS, HALF), lambda m: (m, 0, 0)),
            pl.BlockSpec((1, ROWS, RANK), lambda m: (m, 0, 0)),
        ],
        out_shape=[f32(MATS, ROWS, HALF), f32(MATS, ROWS, HALF), f32(MATS, ROWS, RANK)],
        compiler_params=params(),
        cost_estimate=pl.CostEstimate(flops=400_000_000, bytes_accessed=4_000_000, transcendentals=0),
        name="decode",
    )(place, codes, scales, table, gradient, basis)


def cross_body(place_ref, kept_ref, received_ref, power_ref, pieces_ref):
    place, block = place_ref[0], place_ref[1]
    for m in range(MATS):
        left = jnp.concatenate([kept_ref[m], received_ref[m]], axis=0)
        right = jnp.concatenate([power_ref[place, m], power_ref[1 - place, m]], axis=0)
        product = near_dot(left, right, ((0,), (0,)))
        for h in range(2):
            pieces_ref[16 * m : 16 * m + 16, 32 * h : 32 * h + 32, :] = product[
                :, 128 * h : 128 * h + 128
            ].reshape(16, 32, 128)
    mat = block // 2
    lanes = pl.ds(pl.multiple_of(block % 2 * 128, 128), 128)
    some = jnp.concatenate([power_ref[0, mat, :, lanes], power_ref[1, mat, :, lanes]], axis=0)
    every = jnp.concatenate([power_ref[0, mat], power_ref[1, mat]], axis=0)
    gram = high_dot(some, every, ((0,), (0,)))
    for h in range(2):
        pieces_ref[16 * h : 16 * h + 16, 64:72, :] = gram[:, 128 * h : 128 * h + 128].reshape(
            16, 8, 128
        )


def cross(place, kept, received, power):
    return pl.pallas_call(
        cross_body,
        in_specs=[pl.BlockSpec(memory_space=pltpu.SMEM)]
        + [pl.BlockSpec(memory_space=pltpu.VMEM)] * 3,
        out_specs=pl.BlockSpec(memory_space=pltpu.VMEM),
        out_shape=f32(32, PIECE, 128),
        compiler_params=params(),
        cost_estimate=pl.CostEstimate(flops=800_000_000, bytes_accessed=2_600_000, transcendentals=0),
        name="cross",
    )(place, kept, received, power)


def lane_copy(tile, lane):
    return jnp.take_along_axis(tile, jnp.full((8, 128), lane, jnp.int32), axis=1)


def row_copy(tile, row):
    return jnp.broadcast_to(tile[row : row + 1], (8, 128))


def eliminate(tiles, base):
    sub = lax.broadcasted_iota(jnp.int32, (8, 128), 0)
    tiles = list(tiles)
    done = []
    for t in range(8):
        at = base + 8 * t
        work = [lane_copy(tiles[t], at + i) for i in range(8)] + [tiles[t]]
        steps = []
        rows = [None] * 8
        for p in range(0, 8, 2):
            a = row_copy(work[p], p)
            b = row_copy(work[p + 1], p)
            c = row_copy(work[p + 1], p + 1)
            det = a * c - b * b
            inv_det = 1.0 / det
            ca, cb, cc = a * inv_det, b * inv_det, c * inv_det
            later = sub > p + 1
            left = jnp.where(later, work[p], 0.0)
            right = jnp.where(later, work[p + 1], 0.0)
            step = {}
            for i in range(p + 2, 9):
                x = row_copy(work[i], p)
                y = row_copy(work[i], p + 1)
                step[i] = (cc * x - cb * y, ca * y - cb * x)
                if i == 8:
                    rows[p] = x * lax.rsqrt(a)
                    rows[p + 1] = (y - (b / a) * x) * lax.rsqrt(det / a)
                work[i] = work[i] - (left * step[i][0] + right * step[i][1])
            steps.append(step)
        out = rows[0]
        for p in range(1, 8):
            out = jnp.where(sub == p, rows[p], out)
        done.append(out)
        for u in range(t + 1, 8):
            work = [lane_copy(tiles[u], at + i) for i in range(8)] + [tiles[u]]
            for p in range(0, 8, 2):
                step = steps[p // 2]
                for i in range(p + 2, 9):
                    work[i] = work[i] - (work[p] * step[i][0] + work[p + 1] * step[i][1])
            tiles[u] = work[8]
    return jnp.concatenate(done, axis=0)


def factor_body(gram_ref, inv_ref, state_ref):
    n = BLOCKED
    lane = lax.broadcasted_iota(jnp.int32, (n, 128), 1)
    sub = lax.broadcasted_iota(jnp.int32, (n, 128), 0)
    wide = lax.broadcasted_iota(jnp.int32, (n, RANK), 1)
    deep = lax.broadcasted_iota(jnp.int32, (n, RANK), 0)
    for m in range(MATS):
        for top in range(2):
            for h in range(2):
                state_ref[m, 128 * top : 128 * top + 128, 128 * h : 128 * h + 128] = gram_ref[
                    2 * m + top, 128 * h : 128 * h + 128, :
                ]
    for k in range(RANK // n):
        at = k * n
        base = at % 128
        mine = (lane >= base) & (lane < base + n)
        eye = (jnp.where(lane < n, lane, lane - n) == sub).astype(jnp.float32)
        reduced = []
        for m in range(MATS):
            pair = state_ref[m, at : at + n, at - base : at - base + 128]
            block = jnp.where(mine, pair, eye)
            reduced.append(eliminate([block[8 * t : 8 * t + 8] for t in range(8)], base))
        for m in range(MATS):
            low_inv = jnp.where(mine, 0.0, reduced[m])
            rows = jnp.where(
                (wide >= at) & (wide < at + n),
                (wide - at == deep).astype(jnp.float32),
                state_ref[m, at : at + n, :],
            )
            fresh = high_dot(low_inv, jnp.concatenate([rows, rows], axis=0), ((1,), (0,)))
            inv_ref[m, at : at + n, :] = jnp.where(wide < at + n, fresh, 0.0)
            if k == RANK // n - 1:
                continue
            start = (at + n) // 128 * 128
            upper = jnp.where(wide >= at + n, fresh, 0.0)[:, start:]
            change = high_dot(upper, fresh, ((0,), (0,)))
            for r in range(at + n, RANK, n):
                old = state_ref[m, r : r + n, :]
                old = jnp.where((wide >= at) & (wide < at + n), 0.0, old)
                state_ref[m, r : r + n, :] = old - change[r - start : r - start + n]


def inverse_factor(gram):
    return pl.pallas_call(
        factor_body,
        in_specs=[pl.BlockSpec(memory_space=pltpu.VMEM)],
        out_specs=pl.BlockSpec(memory_space=pltpu.VMEM),
        out_shape=f32(MATS, RANK, RANK),
        scratch_shapes=[pltpu.VMEM((MATS, RANK, RANK), jnp.float32)],
        compiler_params=params(),
        cost_estimate=pl.CostEstimate(
            flops=4_000_000_000, bytes_accessed=1_000_000, transcendentals=0
        ),
        name="inverse_factor",
    )(gram)


def finish_body(
    place_ref, inv_ref, power_ref, own_ref, first_ref, second_ref, kept_ref, sent_ref,
    back_ref, ortho_ref, residual_ref, small_ref,
):
    place = place_ref[0]
    for m in range(MATS):
        factor = inv_ref[m]
        ortho = high_dot(power_ref[place, m], factor, ((1,), (1,)))
        ortho_ref[m] = ortho
        squares = None
        peak = None
        for h in range(2):
            pieces = own_ref[16 * m : 16 * m + 16] if h == 0 else (first_ref, second_ref)[m][...]
            summed = jnp.concatenate(
                [pieces[:, :32].reshape(HALF, 128), pieces[:, 32:64].reshape(HALF, 128)], axis=1
            )
            back = near_dot(summed, factor, ((1,), (1,)))
            at = pl.ds(pl.multiple_of((place + h) % 2 * HALF, HALF), HALF)
            back_ref[m, at, :] = back
            part = jnp.sum(back * back, axis=0, keepdims=True)
            squares = part if squares is None else squares + part
            residual = (kept_ref, sent_ref)[h][m] - (1.0 - momentum_decay) * near_dot(
                ortho, back, ((1,), (1,))
            )
            residual_ref[m, :, at] = residual
            top = jnp.max(jnp.abs(residual), axis=1, keepdims=True)
            peak = top if peak is None else jnp.maximum(peak, top)
        small_ref[2 * m : 2 * m + 1] = squares[:, :128]
        small_ref[2 * m + 1 : 2 * m + 2] = squares[:, 128:]
        small_ref[4 + m : 5 + m] = turned_row(peak)
    small_ref[6:8] = jnp.zeros((2, 128), jnp.float32)


def finish(place, inv, power, own, first, second, kept, sent):
    return pl.pallas_call(
        finish_body,
        in_specs=[pl.BlockSpec(memory_space=pltpu.SMEM)]
        + [pl.BlockSpec(memory_space=pltpu.VMEM)] * 7,
        out_specs=[pl.BlockSpec(memory_space=pltpu.VMEM)] * 4,
        out_shape=[
            f32(MATS, COLS, RANK),
            f32(MATS, ROWS, RANK),
            f32(MATS, ROWS, COLS),
            f32(8, 128),
        ],
        compiler_params=params(),
        cost_estimate=pl.CostEstimate(
            flops=1_300_000_000, bytes_accessed=7_000_000, transcendentals=0
        ),
        name="finish",
    )(place, inv, power, own, first, second, kept, sent)


def outputs_body(
    place_ref, small_ref, back_ref, ortho_ref, residual_ref, weight_ref,
    momentum_ref, peaks_ref, basis_ref, new_weight_ref,
):
    total = small_ref[0]
    for i in range(1, 8):
        total = total + small_ref[i]
    block = place_ref[1]
    for m in range(MATS):
        squares = jnp.concatenate([total[2 * m : 2 * m + 1], total[2 * m + 1 : 2 * m + 2]], axis=1)
        norm = lax.rsqrt(squares + epsilon)
        basis = back_ref[m] * norm
        basis_ref[m] = basis.astype(jnp.bfloat16)
        for b in range(D // BLOCK):
            peaks_ref[m, b : b + 1] = jnp.maximum(
                small_ref[2 * b, 4 + m : 5 + m], small_ref[2 * b + 1, 4 + m : 5 + m]
            )
        mine = jnp.maximum(
            small_ref[2 * block, 4 + m : 5 + m], small_ref[2 * block + 1, 4 + m : 5 + m]
        )
        scale = turned_column(mine) + epsilon
        scale = jnp.concatenate([scale] * (COLS // 128), axis=1)
        momentum_ref[m] = (residual_ref[m] / scale).astype(jnp.bfloat16)
        update = near_dot(ortho_ref[m], basis, ((1,), (1,))) * (D / math.sqrt(RANK))
        new_weight_ref[m] = (weight_ref[m].astype(jnp.float32) - step_size * update).astype(
            jnp.bfloat16
        )


def outputs(place, small, back, ortho, residual, weight):
    return pl.pallas_call(
        outputs_body,
        in_specs=[pl.BlockSpec(memory_space=pltpu.SMEM)]
        + [pl.BlockSpec(memory_space=pltpu.VMEM)] * 5,
        out_specs=[pl.BlockSpec(memory_space=pltpu.VMEM)] * 4,
        out_shape=[
            jax.ShapeDtypeStruct((MATS, ROWS, COLS), jnp.bfloat16),
            f32(MATS, D // BLOCK, ROWS),
            jax.ShapeDtypeStruct((MATS, COLS, RANK), jnp.bfloat16),
            jax.ShapeDtypeStruct((MATS, ROWS, COLS), jnp.bfloat16),
        ],
        compiler_params=params(),
        cost_estimate=pl.CostEstimate(
            flops=500_000_000, bytes_accessed=7_000_000, transcendentals=0
        ),
        name="outputs",
    )(place, small, back, ortho, residual, weight)


def row_shift(step):
    return [(i, i // 8 * 8 + (i + step) % 8) for i in range(64)]


def per_device(codes, scales, table, gradient, weight, basis):
    place = jnp.stack([lax.axis_index("yl"), lax.axis_index("x")]).astype(jnp.int32)
    kept, sent, partial_power = decode(
        place, codes, jnp.swapaxes(scales, 1, 2), table.reshape(2, 128), gradient, basis
    )

    received = lax.ppermute(sent, "yl", [(0, 1), (1, 0)])

    pieces = lax.all_to_all(partial_power.reshape(8, 32, RANK), COLS_AXES, 0, 0, tiled=True)
    piece = jnp.sum(pieces, axis=0)
    power = everyone(piece, GROUP).reshape(2, MATS, ROWS, RANK)

    pieces = lax.all_to_all(cross(place, kept, received, power), OTHERS, 0, 0, tiled=True)
    piece = jnp.sum(pieces, axis=0)
    own = everyone(piece, OTHERS)
    rows_axes = ("zh", "zl", "yh", "yl")
    first = lax.ppermute(own[:16, :64], rows_axes, row_shift(1))
    second = lax.ppermute(own[16:, :64], rows_axes, row_shift(7))
    gram = everyone(own[:, 64:].reshape(RANK, 128), "x")
    inv = inverse_factor(gram)

    back, ortho, residual, small = finish(place, inv, power, own, first, second, kept, sent)
    small = everyone(small, COLS_AXES)
    new_momentum, peaks, new_basis, new_weight = outputs(
        place, small, back, ortho, residual, weight
    )
    return new_momentum, jnp.swapaxes(peaks, 1, 2), new_basis, new_weight


def solution(mesh):
    axes = ("zh", "zl", "yh", "yl", "x", "core")
    fine = Mesh(mesh.devices.reshape(4, 2, 4, 2, 4, 2), axes)
    rows = axes[:4]
    cols = axes[4:]
    return jax.shard_map(
        per_device,
        mesh=fine,
        in_specs=(
            P(None, rows, cols),
            P(None, rows, None),
            P(),
            P(None, rows, cols),
            P(None, rows, cols),
            P(None, cols, None),
        ),
        out_specs=(
            P(None, rows, cols),
            P(None, rows, None),
            P(None, cols, None),
            P(None, rows, cols),
        ),
        check_vma=False,
    )
```

```python
import math

import jax
import jax.numpy as jnp
from jax import lax
from jax.experimental import pallas as pl
from jax.experimental.pallas import tpu as pltpu
from jax.sharding import Mesh
from jax.sharding import PartitionSpec as P


D = 8192
RANK = 256
BLOCK = 2048
MATS = 2

epsilon = 1e-06
momentum_decay = 0.95
step_size = 0.5

ROWS = 128
COLS = 1024
HALF = COLS // 2
PIECE = 72
BLOCKED = 64
COLS_AXES = ("x", "core")
GROUP = ("yl", "x", "core")
OTHERS = ("zh", "yh")


def f32(*shape):
    return jax.ShapeDtypeStruct(shape, jnp.float32)


def high_dot(a, b, dims):
    return lax.dot_general(
        a, b, (dims, ((), ())), precision=lax.Precision.HIGHEST, preferred_element_type=jnp.float32
    )


def split_dot(a, b):
    total = None
    for _ in range(3):
        term = a.astype(jnp.bfloat16)
        a = a - term.astype(jnp.float32)
        part = jnp.dot(term, b, preferred_element_type=jnp.float32)
        total = part if total is None else total + part
    return total


def near_dot(a, b, dims):
    a_top = a.astype(jnp.bfloat16)
    b_top = b.astype(jnp.bfloat16)
    a_rest = (a - a_top.astype(jnp.float32)).astype(jnp.bfloat16)
    b_rest = (b - b_top.astype(jnp.float32)).astype(jnp.bfloat16)

    def dot(x, y):
        return lax.dot_general(x, y, (dims, ((), ())), preferred_element_type=jnp.float32)

    return dot(a_top, b_top) + (dot(a_top, b_rest) + dot(a_rest, b_top))


def params():
    return pltpu.CompilerParams(vmem_limit_bytes=24 * 1024 * 1024)


def everyone(value, axes):
    count = lax.axis_size(axes)
    copies = jnp.broadcast_to(value, (count, *value.shape))
    return lax.all_to_all(copies, axes, 0, 0, tiled=True)


def turned_row(column):
    return jnp.transpose(jnp.broadcast_to(column, (ROWS, 128)))[0:1]


def turned_column(row):
    return jnp.transpose(jnp.broadcast_to(row, (128, ROWS)))


def decode_body(
    place_ref, codes_hbm, scale_hbm, table_hbm, grad_hbm, basis_hbm,
    kept_ref, sent_ref, power_ref,
    codes_ref, scale_ref, table_ref, grad_ref, basis_ref, small_sems, sems,
):
    place, block = place_ref[0], place_ref[1]
    copies = [
        pltpu.make_async_copy(table_hbm, table_ref, small_sems.at[0]),
        pltpu.make_async_copy(scale_hbm, scale_ref, small_sems.at[1]),
    ]
    for m in range(MATS):
        for i, (source, target) in enumerate(
            ((codes_hbm, codes_ref), (grad_hbm, grad_ref), (basis_hbm, basis_ref))
        ):
            copies.append(pltpu.make_async_copy(source.at[m], target.at[m], sems.at[m, i]))
    for copy in copies:
        copy.start()
    copies[0].wait()
    copies[1].wait()
    low = jnp.broadcast_to(table_ref[0:1], (ROWS, 128))
    high = jnp.broadcast_to(table_ref[1:2], (ROWS, 128))
    for m in range(MATS):
        copies[2 + 3 * m].wait()
        copies[3 + 3 * m].wait()
        scale = turned_column(scale_ref[m, pl.ds(block, 1), :])
        both = []
        for half, out_ref in ((1 - place, sent_ref), (place, kept_ref)):
            pieces = []
            for t in range(HALF // 128):
                lanes = pl.ds(pl.multiple_of(half * HALF + t * 128, 128), 128)
                code = codes_ref[m, :, lanes]
                index = code & 127
                value = jnp.where(
                    code < 128,
                    jnp.take_along_axis(low, index, axis=1),
                    jnp.take_along_axis(high, index, axis=1),
                )
                pieces.append(value * scale + grad_ref[m, :, lanes].astype(jnp.float32))
            piece = jnp.concatenate(pieces, axis=1)
            out_ref[m] = piece
            both.append((half, piece))
        copies[4 + 3 * m].wait()
        parts = [
            split_dot(piece, basis_ref[m, pl.ds(pl.multiple_of(half * HALF, HALF), HALF), :])
            for half, piece in both
        ]
        power_ref[m] = parts[0] + parts[1]


def decode(place, codes, scales, table, gradient, basis):
    return pl.pallas_call(
        decode_body,
        in_specs=[pl.BlockSpec(memory_space=pltpu.SMEM)]
        + [pl.BlockSpec(memory_space=pltpu.HBM)] * 5,
        out_specs=[pl.BlockSpec(memory_space=pltpu.VMEM)] * 3,
        out_shape=[f32(MATS, ROWS, HALF), f32(MATS, ROWS, HALF), f32(MATS, ROWS, RANK)],
        scratch_shapes=[
            pltpu.VMEM(codes.shape, codes.dtype),
            pltpu.VMEM(scales.shape, scales.dtype),
            pltpu.VMEM(table.shape, table.dtype),
            pltpu.VMEM(gradient.shape, gradient.dtype),
            pltpu.VMEM(basis.shape, basis.dtype),
            pltpu.SemaphoreType.DMA((2,)),
            pltpu.SemaphoreType.DMA((MATS, 3)),
        ],
        compiler_params=pltpu.CompilerParams(vmem_limit_bytes=53600 * 1024),
        cost_estimate=pl.CostEstimate(flops=400_000_000, bytes_accessed=4_000_000, transcendentals=0),
        name="decode",
    )(place, codes, scales, table, gradient, basis)


def cross_body(place_ref, kept_ref, received_ref, power_ref, stay_ref, up_ref, down_ref):
    place, block, parity = place_ref[0], place_ref[1], place_ref[2]
    mat = block // 2
    lanes = pl.ds(pl.multiple_of(block % 2 * 128, 128), 128)
    some = jnp.concatenate([power_ref[0, mat, :, lanes], power_ref[1, mat, :, lanes]], axis=0)
    for other in range(2):
        m = parity if other == 0 else 1 - parity
        left = jnp.concatenate([kept_ref[m], received_ref[m]], axis=0)
        right = jnp.concatenate([power_ref[place, m], power_ref[1 - place, m]], axis=0)
        product = near_dot(left, right, ((0,), (0,)))
        wide = pl.ds(pl.multiple_of(m * 128, 128), 128)
        every = jnp.concatenate([power_ref[0, mat, :, wide], power_ref[1, mat, :, wide]], axis=0)
        gram = high_dot(some, every, ((0,), (0,))).reshape(16, 8, 128)
        halves = [product[:, 128 * h : 128 * h + 128].reshape(16, 32, 128) for h in range(2)]
        places = ((stay_ref, 0, 16),) if other == 0 else ((up_ref, 0, 8), (down_ref, 8, 16))
        for ref, start, end in places:
            ref[:, 0:32, :] = halves[0][start:end]
            ref[:, 32:64, :] = halves[1][start:end]
            ref[:, 64:72, :] = gram[start:end]


def cross(place, kept, received, power):
    return pl.pallas_call(
        cross_body,
        in_specs=[pl.BlockSpec(memory_space=pltpu.SMEM)]
        + [pl.BlockSpec(memory_space=pltpu.VMEM)] * 3,
        out_specs=[pl.BlockSpec(memory_space=pltpu.VMEM)] * 3,
        out_shape=[f32(16, PIECE, 128), f32(8, PIECE, 128), f32(8, PIECE, 128)],
        compiler_params=params(),
        cost_estimate=pl.CostEstimate(flops=800_000_000, bytes_accessed=2_600_000, transcendentals=0),
        name="cross",
    )(place, kept, received, power)


def merge_body(stay_ref, low_ref, high_ref, out_ref):
    out_ref[:8] = stay_ref[:8] + low_ref[...]
    out_ref[8:] = stay_ref[8:] + high_ref[...]


def merge(stay, low, high):
    return pl.pallas_call(
        merge_body,
        in_specs=[pl.BlockSpec(memory_space=pltpu.VMEM)] * 3,
        out_specs=pl.BlockSpec(memory_space=pltpu.VMEM),
        out_shape=f32(16, PIECE, 128),
        compiler_params=params(),
        cost_estimate=pl.CostEstimate(flops=150_000, bytes_accessed=1_800_000, transcendentals=0),
        name="merge",
    )(stay, low, high)


def lane_copy(tile, lane):
    return jnp.take_along_axis(tile, jnp.full((8, 128), lane, jnp.int32), axis=1)


def row_copy(tile, row):
    return jnp.broadcast_to(tile[row : row + 1], (8, 128))


def eliminate(tiles, base):
    sub = lax.broadcasted_iota(jnp.int32, (8, 128), 0)
    tiles = list(tiles)
    done = []
    for t in range(8):
        at = base + 8 * t
        work = [lane_copy(tiles[t], at + i) for i in range(8)] + [tiles[t]]
        steps = []
        rows = [None] * 8
        for p in range(0, 8, 2):
            a = row_copy(work[p], p)
            b = row_copy(work[p + 1], p)
            c = row_copy(work[p + 1], p + 1)
            det = a * c - b * b
            inv_det = 1.0 / det
            ca, cb, cc = a * inv_det, b * inv_det, c * inv_det
            later = sub > p + 1
            left = jnp.where(later, work[p], 0.0)
            right = jnp.where(later, work[p + 1], 0.0)
            step = {}
            for i in range(p + 2, 9):
                x = row_copy(work[i], p)
                y = row_copy(work[i], p + 1)
                step[i] = (cc * x - cb * y, ca * y - cb * x)
                if i == 8:
                    rows[p] = x * lax.rsqrt(a)
                    rows[p + 1] = (y - (b / a) * x) * lax.rsqrt(det / a)
                work[i] = work[i] - (left * step[i][0] + right * step[i][1])
            steps.append(step)
        out = rows[0]
        for p in range(1, 8):
            out = jnp.where(sub == p, rows[p], out)
        done.append(out)
        for u in range(t + 1, 8):
            work = [lane_copy(tiles[u], at + i) for i in range(8)] + [tiles[u]]
            for p in range(0, 8, 2):
                step = steps[p // 2]
                for i in range(p + 2, 9):
                    work[i] = work[i] - (work[p] * step[i][0] + work[p + 1] * step[i][1])
            tiles[u] = work[8]
    return jnp.concatenate(done, axis=0)


def factor_body(gram_ref, inv_ref, state_ref):
    n = BLOCKED
    lane = lax.broadcasted_iota(jnp.int32, (n, 128), 1)
    sub = lax.broadcasted_iota(jnp.int32, (n, 128), 0)
    wide = lax.broadcasted_iota(jnp.int32, (n, RANK), 1)
    deep = lax.broadcasted_iota(jnp.int32, (n, RANK), 0)
    for m in range(MATS):
        for top in range(2):
            for h in range(2):
                state_ref[m, 128 * top : 128 * top + 128, 128 * h : 128 * h + 128] = gram_ref[
                    4 * m + 2 * top + h
                ]
    for k in range(RANK // n):
        at = k * n
        base = at % 128
        mine = (lane >= base) & (lane < base + n)
        eye = (jnp.where(lane < n, lane, lane - n) == sub).astype(jnp.float32)
        reduced = []
        for m in range(MATS):
            pair = state_ref[m, at : at + n, at - base : at - base + 128]
            block = jnp.where(mine, pair, eye)
            reduced.append(eliminate([block[8 * t : 8 * t + 8] for t in range(8)], base))
        for m in range(MATS):
            low_inv = jnp.where(mine, 0.0, reduced[m])
            rows = jnp.where(
                (wide >= at) & (wide < at + n),
                (wide - at == deep).astype(jnp.float32),
                state_ref[m, at : at + n, :],
            )
            fresh = high_dot(low_inv, jnp.concatenate([rows, rows], axis=0), ((1,), (0,)))
            inv_ref[m, at : at + n, :] = jnp.where(wide < at + n, fresh, 0.0)
            if k == RANK // n - 1:
                continue
            start = (at + n) // 128 * 128
            upper = jnp.where(wide >= at + n, fresh, 0.0)[:, start:]
            change = high_dot(upper, fresh, ((0,), (0,)))
            for r in range(at + n, RANK, n):
                old = state_ref[m, r : r + n, :]
                old = jnp.where((wide >= at) & (wide < at + n), 0.0, old)
                state_ref[m, r : r + n, :] = old - change[r - start : r - start + n]


def inverse_factor(gram):
    return pl.pallas_call(
        factor_body,
        in_specs=[pl.BlockSpec(memory_space=pltpu.VMEM)],
        out_specs=pl.BlockSpec(memory_space=pltpu.VMEM),
        out_shape=f32(MATS, RANK, RANK),
        scratch_shapes=[pltpu.VMEM((MATS, RANK, RANK), jnp.float32)],
        compiler_params=params(),
        cost_estimate=pl.CostEstimate(
            flops=4_000_000_000, bytes_accessed=1_000_000, transcendentals=0
        ),
        name="inverse_factor",
    )(gram)


def finish_body(
    place_ref, inv_ref, power_ref, own_ref, z_low_ref, z_high_ref, y_ref, yz_low_ref, yz_high_ref,
    kept_ref, sent_ref, back_ref, ortho_ref, residual_ref, small_ref,
):
    place, parity = place_ref[0], place_ref[2]
    small_ref[...] = jnp.zeros((8, 128), jnp.float32)
    for other in range(2):
        m = parity if other == 0 else 1 - parity
        factor = inv_ref[m]
        ortho = high_dot(power_ref[place, m], factor, ((1,), (1,)))
        ortho_ref[m] = ortho
        squares = None
        peak = None
        for h in range(2):
            if other == 0:
                pieces = (own_ref, y_ref)[h][...]
            else:
                low_ref, high_ref = ((z_low_ref, z_high_ref), (yz_low_ref, yz_high_ref))[h]
                pieces = jnp.concatenate([low_ref[...], high_ref[...]], axis=0)
            summed = jnp.concatenate(
                [pieces[:, :32].reshape(HALF, 128), pieces[:, 32:64].reshape(HALF, 128)], axis=1
            )
            back = near_dot(summed, factor, ((1,), (1,)))
            at = pl.ds(pl.multiple_of((place + h) % 2 * HALF, HALF), HALF)
            back_ref[m, at, :] = back
            part = jnp.sum(back * back, axis=0, keepdims=True)
            squares = part if squares is None else squares + part
            residual = (kept_ref, sent_ref)[h][m] - (1.0 - momentum_decay) * near_dot(
                ortho, back, ((1,), (1,))
            )
            residual_ref[m, :, at] = residual
            top = jnp.max(jnp.abs(residual), axis=1, keepdims=True)
            peak = top if peak is None else jnp.maximum(peak, top)
        small_ref[pl.ds(2 * m, 1), :] = squares[:, :128]
        small_ref[pl.ds(2 * m + 1, 1), :] = squares[:, 128:]
        small_ref[pl.ds(4 + m, 1), :] = turned_row(peak)


def finish(place, inv, power, summed, kept, sent):
    return pl.pallas_call(
        finish_body,
        in_specs=[pl.BlockSpec(memory_space=pltpu.SMEM)]
        + [pl.BlockSpec(memory_space=pltpu.VMEM)] * 10,
        out_specs=[pl.BlockSpec(memory_space=pltpu.VMEM)] * 4,
        out_shape=[
            f32(MATS, COLS, RANK),
            f32(MATS, ROWS, RANK),
            f32(MATS, ROWS, COLS),
            f32(8, 128),
        ],
        compiler_params=params(),
        cost_estimate=pl.CostEstimate(
            flops=1_300_000_000, bytes_accessed=7_000_000, transcendentals=0
        ),
        name="finish",
    )(place, inv, power, *summed, kept, sent)


def outputs_body(
    place_ref, small_ref, back_ref, ortho_ref, residual_ref, weight_ref,
    momentum_ref, peaks_ref, basis_ref, new_weight_ref,
):
    total = small_ref[0]
    for i in range(1, 8):
        total = total + small_ref[i]
    block = place_ref[1]
    for m in range(MATS):
        squares = jnp.concatenate([total[2 * m : 2 * m + 1], total[2 * m + 1 : 2 * m + 2]], axis=1)
        norm = lax.rsqrt(squares + epsilon)
        basis = back_ref[m] * norm
        basis_ref[m] = basis.astype(jnp.bfloat16)
        for b in range(D // BLOCK):
            peaks_ref[m, b : b + 1] = jnp.maximum(
                small_ref[2 * b, 4 + m : 5 + m], small_ref[2 * b + 1, 4 + m : 5 + m]
            )
        mine = jnp.maximum(
            small_ref[2 * block, 4 + m : 5 + m], small_ref[2 * block + 1, 4 + m : 5 + m]
        )
        scale = turned_column(mine) + epsilon
        scale = jnp.concatenate([scale] * (COLS // 128), axis=1)
        momentum_ref[m] = (residual_ref[m] / scale).astype(jnp.bfloat16)
        update = near_dot(ortho_ref[m], basis, ((1,), (1,))) * (D / math.sqrt(RANK))
        new_weight_ref[m] = (weight_ref[m].astype(jnp.float32) - step_size * update).astype(
            jnp.bfloat16
        )


def outputs(place, small, back, ortho, residual, weight):
    return pl.pallas_call(
        outputs_body,
        in_specs=[pl.BlockSpec(memory_space=pltpu.SMEM)]
        + [pl.BlockSpec(memory_space=pltpu.VMEM)] * 5,
        out_specs=[pl.BlockSpec(memory_space=pltpu.VMEM)] * 4,
        out_shape=[
            jax.ShapeDtypeStruct((MATS, ROWS, COLS), jnp.bfloat16),
            f32(MATS, D // BLOCK, ROWS),
            jax.ShapeDtypeStruct((MATS, COLS, RANK), jnp.bfloat16),
            jax.ShapeDtypeStruct((MATS, ROWS, COLS), jnp.bfloat16),
        ],
        compiler_params=params(),
        cost_estimate=pl.CostEstimate(
            flops=500_000_000, bytes_accessed=7_000_000, transcendentals=0
        ),
        name="outputs",
    )(place, small, back, ortho, residual, weight)


ROW_AXES = ("zh", "zl", "yh", "yl")


def y_shift(value, step):
    pairs = [(i, i // 8 * 8 + (i + step) % 8) for i in range(64)]
    return lax.ppermute(value, ROW_AXES, pairs)


def z_shift(value, step):
    pairs = [(i, (i + 8 * step) % 64) for i in range(64)]
    return lax.ppermute(value, ROW_AXES, pairs)


def per_device(codes, scales, table, gradient, weight, basis):
    place = jnp.stack([lax.axis_index(axis) for axis in ("yl", "x", "zl")]).astype(jnp.int32)
    kept, sent, partial_power = decode(
        place, codes, jnp.swapaxes(scales, 1, 2), table.reshape(2, 128), gradient, basis
    )

    received = lax.ppermute(sent, "yl", [(0, 1), (1, 0)])

    pieces = lax.all_to_all(partial_power.reshape(8, 32, RANK), COLS_AXES, 0, 0, tiled=True)
    piece = jnp.sum(pieces, axis=0)
    power = everyone(piece, GROUP).reshape(2, MATS, ROWS, RANK)

    stay, up, down = cross(place, kept, received, power)
    low = z_shift(up, 1)
    high = z_shift(down, -1)
    pieces = lax.all_to_all(merge(stay, low, high), OTHERS, 0, 0, tiled=True)
    piece = jnp.sum(pieces, axis=0)
    own = everyone(piece, OTHERS)

    gram = everyone(own[:, 64:].reshape(128, 128), ("x", "zl"))
    z_low = z_shift(own[:8], 1)
    z_high = z_shift(own[8:], -1)
    y = y_shift(own, 1)
    yz_low = y_shift(z_low, -1)
    yz_high = y_shift(z_high, -1)
    inv = inverse_factor(gram)

    back, ortho, residual, small = finish(
        place, inv, power, (own, z_low, z_high, y, yz_low, yz_high), kept, sent
    )
    small = everyone(small, COLS_AXES)
    new_momentum, peaks, new_basis, new_weight = outputs(
        place, small, back, ortho, residual, weight
    )
    return new_momentum, jnp.swapaxes(peaks, 1, 2), new_basis, new_weight


def solution(mesh):
    axes = ("zh", "zl", "yh", "yl", "x", "core")
    fine = Mesh(mesh.devices.reshape(4, 2, 4, 2, 4, 2), axes)
    rows = axes[:4]
    cols = axes[4:]
    return jax.shard_map(
        per_device,
        mesh=fine,
        in_specs=(
            P(None, rows, cols),
            P(None, rows, None),
            P(),
            P(None, rows, cols),
            P(None, rows, cols),
            P(None, cols, None),
        ),
        out_specs=(
            P(None, rows, cols),
            P(None, rows, None),
            P(None, cols, None),
            P(None, rows, cols),
        ),
        check_vma=False,
    )
```

```python
import math

import jax
import jax.numpy as jnp
from jax import lax
from jax.experimental import pallas as pl
from jax.experimental.pallas import tpu as pltpu
from jax.sharding import Mesh
from jax.sharding import PartitionSpec as P


D = 8192
RANK = 256
BLOCK = 2048
MATS = 2

epsilon = 1e-06
momentum_decay = 0.95
step_size = 0.5

ROWS = 128
COLS = 1024
QUARTER = COLS // 4
PIECE = 72
BLOCKED = 64
COLS_AXES = ("x", "core")
GROUP = ("zl", "yl", "x")
OTHERS = ("zh", "yh")


def f32(*shape):
    return jax.ShapeDtypeStruct(shape, jnp.float32)


def high_dot(a, b, dims):
    return lax.dot_general(
        a, b, (dims, ((), ())), precision=lax.Precision.HIGHEST, preferred_element_type=jnp.float32
    )


def split_dot(a, b):
    total = None
    for _ in range(3):
        term = a.astype(jnp.bfloat16)
        a = a - term.astype(jnp.float32)
        part = jnp.dot(term, b, preferred_element_type=jnp.float32)
        total = part if total is None else total + part
    return total


def near_dot(a, b, dims):
    a_top = a.astype(jnp.bfloat16)
    b_top = b.astype(jnp.bfloat16)
    a_rest = (a - a_top.astype(jnp.float32)).astype(jnp.bfloat16)
    b_rest = (b - b_top.astype(jnp.float32)).astype(jnp.bfloat16)

    def dot(x, y):
        return lax.dot_general(x, y, (dims, ((), ())), preferred_element_type=jnp.float32)

    return dot(a_top, b_top) + (dot(a_top, b_rest) + dot(a_rest, b_top))


def params():
    return pltpu.CompilerParams(vmem_limit_bytes=24 * 1024 * 1024)


def everyone(value, axes):
    count = lax.axis_size(axes)
    copies = jnp.broadcast_to(value, (count, *value.shape))
    return lax.all_to_all(copies, axes, 0, 0, tiled=True)


def quarter_of(place_ref, turn):
    y, z = place_ref[0], place_ref[2]
    return 2 * (1 - z if turn // 2 else z) + (1 - y if turn % 2 else y)


def turned_row(column):
    return jnp.transpose(jnp.broadcast_to(column, (ROWS, 128)))[0:1]


def turned_column(row):
    return jnp.transpose(jnp.broadcast_to(row, (128, ROWS)))


def decode_body(
    place_ref, codes_hbm, scale_hbm, table_hbm, grad_hbm, basis_hbm,
    own_ref, y_ref, z_ref, diagonal_ref, power_ref,
    codes_ref, scale_ref, table_ref, grad_ref, basis_ref, small_sems, sems,
):
    block = place_ref[1]
    copies = [
        pltpu.make_async_copy(table_hbm, table_ref, small_sems.at[0]),
        pltpu.make_async_copy(scale_hbm, scale_ref, small_sems.at[1]),
    ]
    for m in range(MATS):
        for i, (source, target) in enumerate(
            ((codes_hbm, codes_ref), (grad_hbm, grad_ref), (basis_hbm, basis_ref))
        ):
            copies.append(pltpu.make_async_copy(source.at[m], target.at[m], sems.at[m, i]))
    for copy in copies:
        copy.start()
    copies[0].wait()
    copies[1].wait()
    low = jnp.broadcast_to(table_ref[0:1], (ROWS, 128))
    high = jnp.broadcast_to(table_ref[1:2], (ROWS, 128))
    for m in range(MATS):
        copies[2 + 3 * m].wait()
        copies[3 + 3 * m].wait()
        scale = turned_column(scale_ref[m, pl.ds(block, 1), :])
        both = []
        for turn, out_ref in enumerate((own_ref, y_ref, z_ref, diagonal_ref)):
            start = quarter_of(place_ref, turn) * QUARTER
            pieces = []
            for t in range(QUARTER // 128):
                lanes = pl.ds(pl.multiple_of(start + t * 128, 128), 128)
                code = codes_ref[m, :, lanes]
                index = code & 127
                value = jnp.where(
                    code < 128,
                    jnp.take_along_axis(low, index, axis=1),
                    jnp.take_along_axis(high, index, axis=1),
                )
                pieces.append(value * scale + grad_ref[m, :, lanes].astype(jnp.float32))
            piece = jnp.concatenate(pieces, axis=1)
            out_ref[m] = piece
            both.append((start, piece))
        copies[4 + 3 * m].wait()
        parts = [
            split_dot(piece, basis_ref[m, pl.ds(pl.multiple_of(start, QUARTER), QUARTER), :])
            for start, piece in both
        ]
        power_ref[m] = (parts[0] + parts[1]) + (parts[2] + parts[3])


def decode(place, codes, scales, table, gradient, basis):
    return pl.pallas_call(
        decode_body,
        in_specs=[pl.BlockSpec(memory_space=pltpu.SMEM)]
        + [pl.BlockSpec(memory_space=pltpu.HBM)] * 5,
        out_specs=[pl.BlockSpec(memory_space=pltpu.VMEM)] * 5,
        out_shape=[f32(MATS, ROWS, QUARTER)] * 4 + [f32(MATS, ROWS, RANK)],
        scratch_shapes=[
            pltpu.VMEM(codes.shape, codes.dtype),
            pltpu.VMEM(scales.shape, scales.dtype),
            pltpu.VMEM(table.shape, table.dtype),
            pltpu.VMEM(gradient.shape, gradient.dtype),
            pltpu.VMEM(basis.shape, basis.dtype),
            pltpu.SemaphoreType.DMA((2,)),
            pltpu.SemaphoreType.DMA((MATS, 3)),
        ],
        compiler_params=pltpu.CompilerParams(vmem_limit_bytes=53600 * 1024),
        cost_estimate=pl.CostEstimate(flops=400_000_000, bytes_accessed=4_000_000, transcendentals=0),
        name="decode",
    )(place, codes, scales, table, gradient, basis)


def stack_rows_body(own_ref, y_ref, z_ref, diagonal_ref, top_ref, rest_ref):
    for turn, ref in enumerate((own_ref, y_ref, z_ref, diagonal_ref)):
        for m in range(MATS):
            value = ref[m]
            top = value.astype(jnp.bfloat16)
            at = slice(ROWS * turn, ROWS * turn + ROWS)
            top_ref[m, at, :] = top
            rest_ref[m, at, :] = (value - top.astype(jnp.float32)).astype(jnp.bfloat16)


def stack_rows(*blocks):
    return pl.pallas_call(
        stack_rows_body,
        in_specs=[pl.BlockSpec(memory_space=pltpu.VMEM)] * 4,
        out_specs=[pl.BlockSpec(memory_space=pltpu.VMEM)] * 2,
        out_shape=[jax.ShapeDtypeStruct((MATS, 4 * ROWS, QUARTER), jnp.bfloat16)] * 2,
        compiler_params=params(),
        cost_estimate=pl.CostEstimate(flops=800_000, bytes_accessed=2_000_000, transcendentals=0),
        name="stack_rows",
    )(*blocks)


def cross_body(
    place_ref, top_ref, rest_ref, near_ref, far_ref,
    pieces_ref, own_power_ref, power_ref,
):
    block, core = place_ref[1], place_ref[3]
    for neighbour in range(4):
        for x in range(4):
            power_ref[neighbour, 2 * x + core] = near_ref[4 * neighbour + x]
            power_ref[neighbour, 2 * x + 1 - core] = far_ref[4 * neighbour + x]
    neighbours = [quarter_of(place_ref, turn) for turn in range(4)]
    for m in range(MATS):
        rows = [power_ref[n, 4 * m : 4 * m + 4].reshape(ROWS, RANK) for n in neighbours]
        own_power_ref[m] = rows[0]
        right = jnp.concatenate(rows, axis=0)
        right_top = right.astype(jnp.bfloat16)
        right_rest = (right - right_top.astype(jnp.float32)).astype(jnp.bfloat16)
        product = low_dot(top_ref[m], right_top) + (
            low_dot(top_ref[m], right_rest) + low_dot(rest_ref[m], right_top)
        )
        for h in range(2):
            pieces_ref[8 * m : 8 * m + 8, 32 * h : 32 * h + 32, :] = product[
                :, 128 * h : 128 * h + 128
            ].reshape(8, 32, 128)
    mat = pl.ds(block // 2 * 4, 4)
    sides = []
    for part in (block % 2, core):
        lanes = pl.ds(pl.multiple_of(part * 128, 128), 128)
        sides.append(
            jnp.concatenate(
                [power_ref[n, mat, :, lanes].reshape(ROWS, 128) for n in range(4)], axis=0
            )
        )
    pieces_ref[:, 64:72, :] = high_dot(sides[0], sides[1], ((0,), (0,))).reshape(16, 8, 128)


def low_dot(a, b):
    return lax.dot_general(a, b, (((0,), (0,)), ((), ())), preferred_element_type=jnp.float32)


def cross(place, stacked, near, far):
    return pl.pallas_call(
        cross_body,
        in_specs=[pl.BlockSpec(memory_space=pltpu.SMEM)]
        + [pl.BlockSpec(memory_space=pltpu.VMEM)] * 4,
        out_specs=[pl.BlockSpec(memory_space=pltpu.VMEM)] * 2,
        out_shape=[f32(16, PIECE, 128), f32(MATS, ROWS, RANK)],
        scratch_shapes=[pltpu.VMEM((4, 8, 32, RANK), jnp.float32)],
        compiler_params=params(),
        cost_estimate=pl.CostEstimate(flops=800_000_000, bytes_accessed=2_600_000, transcendentals=0),
        name="cross",
    )(place, *stacked, near, far)


def lane_copy(tile, lane):
    return jnp.take_along_axis(tile, jnp.full((8, 128), lane, jnp.int32), axis=1)


def row_copy(tile, row):
    return jnp.broadcast_to(tile[row : row + 1], (8, 128))


def eliminate(tiles, base):
    sub = lax.broadcasted_iota(jnp.int32, (8, 128), 0)
    tiles = list(tiles)
    done = []
    for t in range(8):
        at = base + 8 * t
        work = [lane_copy(tiles[t], at + i) for i in range(8)] + [tiles[t]]
        steps = []
        rows = [None] * 8
        for p in range(0, 8, 2):
            a = row_copy(work[p], p)
            b = row_copy(work[p + 1], p)
            c = row_copy(work[p + 1], p + 1)
            det = a * c - b * b
            inv_det = 1.0 / det
            ca, cb, cc = a * inv_det, b * inv_det, c * inv_det
            later = sub > p + 1
            left = jnp.where(later, work[p], 0.0)
            right = jnp.where(later, work[p + 1], 0.0)
            step = {}
            for i in range(p + 2, 9):
                x = row_copy(work[i], p)
                y = row_copy(work[i], p + 1)
                step[i] = (cc * x - cb * y, ca * y - cb * x)
                if i == 8:
                    rows[p] = x * lax.rsqrt(a)
                    rows[p + 1] = (y - (b / a) * x) * lax.rsqrt(det / a)
                work[i] = work[i] - (left * step[i][0] + right * step[i][1])
            steps.append(step)
        out = rows[0]
        for p in range(1, 8):
            out = jnp.where(sub == p, rows[p], out)
        done.append(out)
        for u in range(t + 1, 8):
            work = [lane_copy(tiles[u], at + i) for i in range(8)] + [tiles[u]]
            for p in range(0, 8, 2):
                step = steps[p // 2]
                for i in range(p + 2, 9):
                    work[i] = work[i] - (work[p] * step[i][0] + work[p + 1] * step[i][1])
            tiles[u] = work[8]
    return jnp.concatenate(done, axis=0)


def factor_body(gram_ref, inv_ref, state_ref):
    n = BLOCKED
    lane = lax.broadcasted_iota(jnp.int32, (n, 128), 1)
    sub = lax.broadcasted_iota(jnp.int32, (n, 128), 0)
    wide = lax.broadcasted_iota(jnp.int32, (n, RANK), 1)
    deep = lax.broadcasted_iota(jnp.int32, (n, RANK), 0)
    for m in range(MATS):
        for top in range(2):
            for h in range(2):
                state_ref[m, 128 * top : 128 * top + 128, 128 * h : 128 * h + 128] = gram_ref[
                    4 * m + 2 * top + h
                ]
    for k in range(RANK // n):
        at = k * n
        base = at % 128
        mine = (lane >= base) & (lane < base + n)
        eye = (jnp.where(lane < n, lane, lane - n) == sub).astype(jnp.float32)
        reduced = []
        for m in range(MATS):
            pair = state_ref[m, at : at + n, at - base : at - base + 128]
            block = jnp.where(mine, pair, eye)
            reduced.append(eliminate([block[8 * t : 8 * t + 8] for t in range(8)], base))
        for m in range(MATS):
            low_inv = jnp.where(mine, 0.0, reduced[m])
            rows = jnp.where(
                (wide >= at) & (wide < at + n),
                (wide - at == deep).astype(jnp.float32),
                state_ref[m, at : at + n, :],
            )
            fresh = high_dot(low_inv, jnp.concatenate([rows, rows], axis=0), ((1,), (0,)))
            inv_ref[m, at : at + n, :] = jnp.where(wide < at + n, fresh, 0.0)
            if k == RANK // n - 1:
                continue
            start = (at + n) // 128 * 128
            upper = jnp.where(wide >= at + n, fresh, 0.0)[:, start:]
            change = high_dot(upper, fresh, ((0,), (0,)))
            for r in range(at + n, RANK, n):
                old = state_ref[m, r : r + n, :]
                old = jnp.where((wide >= at) & (wide < at + n), 0.0, old)
                state_ref[m, r : r + n, :] = old - change[r - start : r - start + n]


def inverse_factor(gram):
    return pl.pallas_call(
        factor_body,
        in_specs=[pl.BlockSpec(memory_space=pltpu.VMEM)],
        out_specs=pl.BlockSpec(memory_space=pltpu.VMEM),
        out_shape=f32(MATS, RANK, RANK),
        scratch_shapes=[pltpu.VMEM((MATS, RANK, RANK), jnp.float32)],
        compiler_params=params(),
        cost_estimate=pl.CostEstimate(
            flops=4_000_000_000, bytes_accessed=1_000_000, transcendentals=0
        ),
        name="inverse_factor",
    )(gram)


def finish_body(
    place_ref, inv_ref, power_ref, own_ref, y_ref, z_ref, diagonal_ref,
    own_buffer_ref, y_buffer_ref, z_buffer_ref, diagonal_buffer_ref,
    back_ref, ortho_ref, residual_ref, small_ref,
):
    summed_refs = (own_ref, y_ref, z_ref, diagonal_ref)
    buffer_refs = (own_buffer_ref, y_buffer_ref, z_buffer_ref, diagonal_buffer_ref)
    small_ref[6:8] = jnp.zeros((2, 128), jnp.float32)
    for m in range(MATS):
        factor = inv_ref[m]
        ortho = high_dot(power_ref[m], factor, ((1,), (1,)))
        ortho_ref[m] = ortho
        squares = None
        peak = None
        for turn in range(4):
            pieces = summed_refs[turn][8 * m : 8 * m + 8]
            summed = jnp.concatenate(
                [pieces[:, :32].reshape(QUARTER, 128), pieces[:, 32:64].reshape(QUARTER, 128)],
                axis=1,
            )
            back = near_dot(summed, factor, ((1,), (1,)))
            at = pl.ds(pl.multiple_of(quarter_of(place_ref, turn) * QUARTER, QUARTER), QUARTER)
            back_ref[m, at, :] = back
            part = jnp.sum(back * back, axis=0, keepdims=True)
            squares = part if squares is None else squares + part
            residual = buffer_refs[turn][m] - (1.0 - momentum_decay) * near_dot(
                ortho, back, ((1,), (1,))
            )
            residual_ref[m, :, at] = residual
            top = jnp.max(jnp.abs(residual), axis=1, keepdims=True)
            peak = top if peak is None else jnp.maximum(peak, top)
        small_ref[2 * m : 2 * m + 1] = squares[:, :128]
        small_ref[2 * m + 1 : 2 * m + 2] = squares[:, 128:]
        small_ref[4 + m : 5 + m] = turned_row(peak)


def finish(place, inv, power, summed, blocks):
    return pl.pallas_call(
        finish_body,
        in_specs=[pl.BlockSpec(memory_space=pltpu.SMEM)]
        + [pl.BlockSpec(memory_space=pltpu.VMEM)] * 10,
        out_specs=[pl.BlockSpec(memory_space=pltpu.VMEM)] * 4,
        out_shape=[
            f32(MATS, COLS, RANK),
            f32(MATS, ROWS, RANK),
            f32(MATS, ROWS, COLS),
            f32(8, 128),
        ],
        compiler_params=params(),
        cost_estimate=pl.CostEstimate(
            flops=1_300_000_000, bytes_accessed=7_000_000, transcendentals=0
        ),
        name="finish",
    )(place, inv, power, *summed, *blocks)


def outputs_body(
    place_ref, small_ref, back_ref, ortho_ref, residual_ref, weight_ref,
    momentum_ref, peaks_ref, basis_ref, new_weight_ref,
):
    total = small_ref[0]
    for i in range(1, 8):
        total = total + small_ref[i]
    block = place_ref[1]
    for m in range(MATS):
        squares = jnp.concatenate([total[2 * m : 2 * m + 1], total[2 * m + 1 : 2 * m + 2]], axis=1)
        norm = lax.rsqrt(squares + epsilon)
        basis = back_ref[m] * norm
        basis_ref[m] = basis.astype(jnp.bfloat16)
        for b in range(D // BLOCK):
            peaks_ref[m, b : b + 1] = jnp.maximum(
                small_ref[2 * b, 4 + m : 5 + m], small_ref[2 * b + 1, 4 + m : 5 + m]
            )
        mine = jnp.maximum(
            small_ref[2 * block, 4 + m : 5 + m], small_ref[2 * block + 1, 4 + m : 5 + m]
        )
        scale = turned_column(mine) + epsilon
        scale = jnp.concatenate([scale] * (COLS // 128), axis=1)
        momentum_ref[m] = (residual_ref[m] / scale).astype(jnp.bfloat16)
        update = near_dot(ortho_ref[m], basis, ((1,), (1,))) * (D / math.sqrt(RANK))
        new_weight_ref[m] = (weight_ref[m].astype(jnp.float32) - step_size * update).astype(
            jnp.bfloat16
        )


def outputs(place, small, back, ortho, residual, weight):
    return pl.pallas_call(
        outputs_body,
        in_specs=[pl.BlockSpec(memory_space=pltpu.SMEM)]
        + [pl.BlockSpec(memory_space=pltpu.VMEM)] * 5,
        out_specs=[pl.BlockSpec(memory_space=pltpu.VMEM)] * 4,
        out_shape=[
            jax.ShapeDtypeStruct((MATS, ROWS, COLS), jnp.bfloat16),
            f32(MATS, D // BLOCK, ROWS),
            jax.ShapeDtypeStruct((MATS, COLS, RANK), jnp.bfloat16),
            jax.ShapeDtypeStruct((MATS, ROWS, COLS), jnp.bfloat16),
        ],
        compiler_params=params(),
        cost_estimate=pl.CostEstimate(
            flops=500_000_000, bytes_accessed=7_000_000, transcendentals=0
        ),
        name="outputs",
    )(place, small, back, ortho, residual, weight)


ROW_AXES = ("zh", "zl", "yh", "yl")


def shift(value, z_step, y_step):
    pairs = [
        (z * 8 + y, (z + z_step) % 8 * 8 + (y + y_step) % 8) for z in range(8) for y in range(8)
    ]
    return lax.ppermute(value, ROW_AXES, pairs)


def swap(value, z_flip, y_flip):
    pairs = [(z * 8 + y, (z ^ z_flip) * 8 + (y ^ y_flip)) for z in range(8) for y in range(8)]
    return lax.ppermute(value, ROW_AXES, pairs)


def per_device(codes, scales, table, gradient, weight, basis):
    place = jnp.stack([lax.axis_index(axis) for axis in ("yl", "x", "zl", "core")])
    place = place.astype(jnp.int32)
    *blocks, partial_power = decode(
        place, codes, jnp.swapaxes(scales, 1, 2), table.reshape(2, 128), gradient, basis
    )

    from_y = swap(blocks[1], 0, 1)
    from_z = swap(blocks[2], 1, 0)
    from_diagonal = swap(blocks[3], 1, 1)

    pieces = lax.all_to_all(partial_power.reshape(8, 32, RANK), COLS_AXES, 0, 0, tiled=True)
    piece = jnp.sum(pieces, axis=0)
    near = everyone(piece, GROUP)
    far = lax.ppermute(near, "core", [(0, 1), (1, 0)])

    stacked = stack_rows(blocks[0], from_y, from_z, from_diagonal)
    pieces, power = cross(place, stacked, near, far)
    pieces = lax.all_to_all(pieces, OTHERS, 0, 0, tiled=True)
    piece = jnp.sum(pieces, axis=0)
    own = everyone(piece, OTHERS)
    y = shift(own, 0, 1)
    z = shift(own, 1, 0)
    diagonal = shift(own, -1, -1)
    gram = everyone(own[:, 64:].reshape(128, 128), COLS_AXES)
    inv = inverse_factor(gram)

    back, ortho, residual, small = finish(place, inv, power, (own, y, z, diagonal), blocks)
    small = everyone(small, COLS_AXES)
    new_momentum, peaks, new_basis, new_weight = outputs(
        place, small, back, ortho, residual, weight
    )
    return new_momentum, jnp.swapaxes(peaks, 1, 2), new_basis, new_weight


def solution(mesh):
    axes = ("zh", "zl", "yh", "yl", "x", "core")
    fine = Mesh(mesh.devices.reshape(4, 2, 4, 2, 4, 2), axes)
    rows = axes[:4]
    cols = axes[4:]
    return jax.shard_map(
        per_device,
        mesh=fine,
        in_specs=(
            P(None, rows, cols),
            P(None, rows, None),
            P(),
            P(None, rows, cols),
            P(None, rows, cols),
            P(None, cols, None),
        ),
        out_specs=(
            P(None, rows, cols),
            P(None, rows, None),
            P(None, cols, None),
            P(None, rows, cols),
        ),
        check_vma=False,
    )
```

```python
import math

import jax
import jax.numpy as jnp
from jax import lax
from jax.experimental import pallas as pl
from jax.experimental.pallas import tpu as pltpu
from jax.sharding import Mesh
from jax.sharding import PartitionSpec as P


D = 8192
RANK = 256
BLOCK = 2048
MATS = 2

epsilon = 1e-06
momentum_decay = 0.95
step_size = 0.5

ROWS = 128
COLS = 1024
QUARTER = COLS // 4
PIECE = 72
BLOCKED = 64
COLS_AXES = ("x", "core")
GROUP = ("zl", "yl", "x")
OTHERS = ("zh", "yh")


def f32(*shape):
    return jax.ShapeDtypeStruct(shape, jnp.float32)


def high_dot(a, b, dims):
    return lax.dot_general(
        a, b, (dims, ((), ())), precision=lax.Precision.HIGHEST, preferred_element_type=jnp.float32
    )


def split_dot(a, b):
    total = None
    for _ in range(3):
        term = a.astype(jnp.bfloat16)
        a = a - term.astype(jnp.float32)
        part = jnp.dot(term, b, preferred_element_type=jnp.float32)
        total = part if total is None else total + part
    return total


def near_dot(a, b, dims):
    a_top = a.astype(jnp.bfloat16)
    b_top = b.astype(jnp.bfloat16)
    a_rest = (a - a_top.astype(jnp.float32)).astype(jnp.bfloat16)
    b_rest = (b - b_top.astype(jnp.float32)).astype(jnp.bfloat16)

    def dot(x, y):
        return lax.dot_general(x, y, (dims, ((), ())), preferred_element_type=jnp.float32)

    return dot(a_top, b_top) + (dot(a_top, b_rest) + dot(a_rest, b_top))


def params():
    return pltpu.CompilerParams(vmem_limit_bytes=24 * 1024 * 1024)


def everyone(value, axes):
    count = lax.axis_size(axes)
    copies = jnp.broadcast_to(value, (count, *value.shape))
    return lax.all_to_all(copies, axes, 0, 0, tiled=True)


def quarter_of(place_ref, turn):
    y, z = place_ref[0], place_ref[2]
    return 2 * (1 - z if turn // 2 else z) + (1 - y if turn % 2 else y)


def turned_row(column):
    return jnp.transpose(jnp.broadcast_to(column, (ROWS, 128)))[0:1]


def turned_column(row):
    return jnp.transpose(jnp.broadcast_to(row, (128, ROWS)))


def decode_body(
    place_ref, codes_hbm, small_ref, grad_hbm, basis_hbm,
    own_ref, y_ref, z_ref, diagonal_ref, power_ref,
    codes_ref, grad_ref, basis_ref, sems,
):
    block = place_ref[1]
    arrays = ((codes_hbm, codes_ref), (grad_hbm, grad_ref), (basis_hbm, basis_ref))
    copies = {
        (m, i): pltpu.make_async_copy(source.at[m], target.at[m], sems.at[m, i])
        for m in range(MATS)
        for i, (source, target) in enumerate(arrays)
    }
    for m, i in ((0, 0), (0, 1), (1, 0), (1, 1), (0, 2), (1, 2)):
        copies[m, i].start()
    low = jnp.broadcast_to(small_ref[8:9], (ROWS, 128))
    high = jnp.broadcast_to(small_ref[9:10], (ROWS, 128))
    for m in range(MATS):
        copies[m, 0].wait()
        copies[m, 1].wait()
        scale = turned_column(small_ref[pl.ds(4 * m + block, 1), :])
        both = []
        for turn, out_ref in enumerate((own_ref, y_ref, z_ref, diagonal_ref)):
            start = quarter_of(place_ref, turn) * QUARTER
            pieces = []
            for t in range(QUARTER // 128):
                lanes = pl.ds(pl.multiple_of(start + t * 128, 128), 128)
                code = codes_ref[m, :, lanes]
                index = code & 127
                value = jnp.where(
                    code < 128,
                    jnp.take_along_axis(low, index, axis=1),
                    jnp.take_along_axis(high, index, axis=1),
                )
                pieces.append(value * scale + grad_ref[m, :, lanes].astype(jnp.float32))
            piece = jnp.concatenate(pieces, axis=1)
            out_ref[m] = piece
            both.append((start, piece))
        copies[m, 2].wait()
        parts = [
            split_dot(piece, basis_ref[m, pl.ds(pl.multiple_of(start, QUARTER), QUARTER), :])
            for start, piece in both
        ]
        power_ref[m] = (parts[0] + parts[1]) + (parts[2] + parts[3])


def decode(place, codes, small, gradient, basis):
    return pl.pallas_call(
        decode_body,
        in_specs=[
            pl.BlockSpec(memory_space=pltpu.SMEM),
            pl.BlockSpec(memory_space=pltpu.HBM),
            pl.BlockSpec(memory_space=pltpu.VMEM),
            pl.BlockSpec(memory_space=pltpu.HBM),
            pl.BlockSpec(memory_space=pltpu.HBM),
        ],
        out_specs=[pl.BlockSpec(memory_space=pltpu.VMEM)] * 5,
        out_shape=[f32(MATS, ROWS, QUARTER)] * 4 + [f32(MATS, ROWS, RANK)],
        scratch_shapes=[
            pltpu.VMEM(codes.shape, codes.dtype),
            pltpu.VMEM(gradient.shape, gradient.dtype),
            pltpu.VMEM(basis.shape, basis.dtype),
            pltpu.SemaphoreType.DMA((MATS, 3)),
        ],
        compiler_params=pltpu.CompilerParams(vmem_limit_bytes=53600 * 1024),
        cost_estimate=pl.CostEstimate(flops=400_000_000, bytes_accessed=4_000_000, transcendentals=0),
        name="decode",
    )(place, codes, small, gradient, basis)


def stack_rows_body(first_ref, second_ref, top_ref, rest_ref):
    for i, ref in enumerate((first_ref, second_ref)):
        for m in range(MATS):
            value = ref[m]
            top = value.astype(jnp.bfloat16)
            at = slice(ROWS * i, ROWS * i + ROWS)
            top_ref[m, at, :] = top
            rest_ref[m, at, :] = (value - top.astype(jnp.float32)).astype(jnp.bfloat16)


def stack_rows(first, second):
    return pl.pallas_call(
        stack_rows_body,
        in_specs=[pl.BlockSpec(memory_space=pltpu.VMEM)] * 2,
        out_specs=[pl.BlockSpec(memory_space=pltpu.VMEM)] * 2,
        out_shape=[jax.ShapeDtypeStruct((MATS, 2 * ROWS, QUARTER), jnp.bfloat16)] * 2,
        compiler_params=params(),
        cost_estimate=pl.CostEstimate(flops=400_000, bytes_accessed=1_000_000, transcendentals=0),
        name="stack_rows",
    )(first, second)


def cross_body(
    place_ref, near_top_ref, near_rest_ref, far_top_ref, far_rest_ref, near_ref, far_ref,
    pieces_ref, own_power_ref, power_ref,
):
    block, core = place_ref[1], place_ref[3]
    for neighbour in range(4):
        for x in range(4):
            power_ref[neighbour, 2 * x + core] = near_ref[4 * neighbour + x]
            power_ref[neighbour, 2 * x + 1 - core] = far_ref[4 * neighbour + x]
    neighbours = [quarter_of(place_ref, turn) for turn in range(4)]
    for m in range(MATS):
        rows = [power_ref[n, 4 * m : 4 * m + 4].reshape(ROWS, RANK) for n in neighbours]
        own_power_ref[m] = rows[0]
        right = jnp.concatenate(rows, axis=0)
        right_top = right.astype(jnp.bfloat16)
        right_rest = (right - right_top.astype(jnp.float32)).astype(jnp.bfloat16)
        top = jnp.concatenate([near_top_ref[m], far_top_ref[m]], axis=0)
        rest = jnp.concatenate([near_rest_ref[m], far_rest_ref[m]], axis=0)
        product = low_dot(top, right_top) + (low_dot(top, right_rest) + low_dot(rest, right_top))
        for h in range(2):
            pieces_ref[8 * m : 8 * m + 8, 32 * h : 32 * h + 32, :] = product[
                :, 128 * h : 128 * h + 128
            ].reshape(8, 32, 128)
    mat = pl.ds(block // 2 * 4, 4)
    sides = []
    for part in (block % 2, core):
        lanes = pl.ds(pl.multiple_of(part * 128, 128), 128)
        sides.append(
            jnp.concatenate(
                [power_ref[n, mat, :, lanes].reshape(ROWS, 128) for n in range(4)], axis=0
            )
        )
    pieces_ref[:, 64:72, :] = high_dot(sides[0], sides[1], ((0,), (0,))).reshape(16, 8, 128)


def low_dot(a, b):
    return lax.dot_general(a, b, (((0,), (0,)), ((), ())), preferred_element_type=jnp.float32)


def cross(place, stacked, near, far):
    return pl.pallas_call(
        cross_body,
        in_specs=[pl.BlockSpec(memory_space=pltpu.SMEM)]
        + [pl.BlockSpec(memory_space=pltpu.VMEM)] * 6,
        out_specs=[pl.BlockSpec(memory_space=pltpu.VMEM)] * 2,
        out_shape=[f32(16, PIECE, 128), f32(MATS, ROWS, RANK)],
        scratch_shapes=[pltpu.VMEM((4, 8, 32, RANK), jnp.float32)],
        compiler_params=params(),
        cost_estimate=pl.CostEstimate(flops=800_000_000, bytes_accessed=2_600_000, transcendentals=0),
        name="cross",
    )(place, *stacked, near, far)


def lane_copy(tile, lane):
    return jnp.take_along_axis(tile, jnp.full((8, 128), lane, jnp.int32), axis=1)


def row_copy(tile, row):
    return jnp.broadcast_to(tile[row : row + 1], (8, 128))


def eliminate(tiles, base):
    sub = lax.broadcasted_iota(jnp.int32, (8, 128), 0)
    tiles = list(tiles)
    done = []
    for t in range(8):
        at = base + 8 * t
        work = [lane_copy(tiles[t], at + i) for i in range(8)] + [tiles[t]]
        steps = []
        rows = [None] * 8
        for p in range(0, 8, 2):
            a = row_copy(work[p], p)
            b = row_copy(work[p + 1], p)
            c = row_copy(work[p + 1], p + 1)
            det = a * c - b * b
            inv_det = 1.0 / det
            ca, cb, cc = a * inv_det, b * inv_det, c * inv_det
            later = sub > p + 1
            left = jnp.where(later, work[p], 0.0)
            right = jnp.where(later, work[p + 1], 0.0)
            step = {}
            for i in range(p + 2, 9):
                x = row_copy(work[i], p)
                y = row_copy(work[i], p + 1)
                step[i] = (cc * x - cb * y, ca * y - cb * x)
                if i == 8:
                    rows[p] = x * lax.rsqrt(a)
                    rows[p + 1] = (y - (b / a) * x) * lax.rsqrt(det / a)
                work[i] = work[i] - (left * step[i][0] + right * step[i][1])
            steps.append(step)
        out = rows[0]
        for p in range(1, 8):
            out = jnp.where(sub == p, rows[p], out)
        done.append(out)
        for u in range(t + 1, 8):
            work = [lane_copy(tiles[u], at + i) for i in range(8)] + [tiles[u]]
            for p in range(0, 8, 2):
                step = steps[p // 2]
                for i in range(p + 2, 9):
                    work[i] = work[i] - (work[p] * step[i][0] + work[p + 1] * step[i][1])
            tiles[u] = work[8]
    return jnp.concatenate(done, axis=0)


def factor_body(gram_ref, inv_ref, state_ref):
    n = BLOCKED
    lane = lax.broadcasted_iota(jnp.int32, (n, 128), 1)
    sub = lax.broadcasted_iota(jnp.int32, (n, 128), 0)
    wide = lax.broadcasted_iota(jnp.int32, (n, RANK), 1)
    deep = lax.broadcasted_iota(jnp.int32, (n, RANK), 0)
    for m in range(MATS):
        for top in range(2):
            for h in range(2):
                state_ref[m, 128 * top : 128 * top + 128, 128 * h : 128 * h + 128] = gram_ref[
                    4 * m + 2 * top + h
                ]
    for k in range(RANK // n):
        at = k * n
        base = at % 128
        mine = (lane >= base) & (lane < base + n)
        eye = (jnp.where(lane < n, lane, lane - n) == sub).astype(jnp.float32)
        reduced = []
        for m in range(MATS):
            pair = state_ref[m, at : at + n, at - base : at - base + 128]
            block = jnp.where(mine, pair, eye)
            reduced.append(eliminate([block[8 * t : 8 * t + 8] for t in range(8)], base))
        for m in range(MATS):
            low_inv = jnp.where(mine, 0.0, reduced[m])
            rows = jnp.where(
                (wide >= at) & (wide < at + n),
                (wide - at == deep).astype(jnp.float32),
                state_ref[m, at : at + n, :],
            )
            fresh = high_dot(low_inv, jnp.concatenate([rows, rows], axis=0), ((1,), (0,)))
            inv_ref[m, at : at + n, :] = jnp.where(wide < at + n, fresh, 0.0)
            if k == RANK // n - 1:
                continue
            start = (at + n) // 128 * 128
            upper = jnp.where(wide >= at + n, fresh, 0.0)[:, start:]
            change = high_dot(upper, fresh, ((0,), (0,)))
            for r in range(at + n, RANK, n):
                old = state_ref[m, r : r + n, :]
                old = jnp.where((wide >= at) & (wide < at + n), 0.0, old)
                state_ref[m, r : r + n, :] = old - change[r - start : r - start + n]


def inverse_factor(gram):
    return pl.pallas_call(
        factor_body,
        in_specs=[pl.BlockSpec(memory_space=pltpu.VMEM)],
        out_specs=pl.BlockSpec(memory_space=pltpu.VMEM),
        out_shape=f32(MATS, RANK, RANK),
        scratch_shapes=[pltpu.VMEM((MATS, RANK, RANK), jnp.float32)],
        compiler_params=params(),
        cost_estimate=pl.CostEstimate(
            flops=4_000_000_000, bytes_accessed=1_000_000, transcendentals=0
        ),
        name="inverse_factor",
    )(gram)


def finish_body(
    place_ref, inv_ref, power_ref, own_ref, y_ref, z_ref, diagonal_ref,
    own_buffer_ref, y_buffer_ref, z_buffer_ref, diagonal_buffer_ref,
    back_ref, ortho_ref, residual_ref, small_ref,
):
    summed_refs = (own_ref, y_ref, z_ref, diagonal_ref)
    buffer_refs = (own_buffer_ref, y_buffer_ref, z_buffer_ref, diagonal_buffer_ref)
    small_ref[6:8] = jnp.zeros((2, 128), jnp.float32)
    for m in range(MATS):
        factor = inv_ref[m]
        ortho = high_dot(power_ref[m], factor, ((1,), (1,)))
        ortho_ref[m] = ortho
        squares = None
        peak = None
        for turn in range(4):
            pieces = summed_refs[turn][8 * m : 8 * m + 8]
            summed = jnp.concatenate(
                [pieces[:, :32].reshape(QUARTER, 128), pieces[:, 32:64].reshape(QUARTER, 128)],
                axis=1,
            )
            back = near_dot(summed, factor, ((1,), (1,)))
            at = pl.ds(pl.multiple_of(quarter_of(place_ref, turn) * QUARTER, QUARTER), QUARTER)
            back_ref[m, at, :] = back
            part = jnp.sum(back * back, axis=0, keepdims=True)
            squares = part if squares is None else squares + part
            residual = buffer_refs[turn][m] - (1.0 - momentum_decay) * near_dot(
                ortho, back, ((1,), (1,))
            )
            residual_ref[m, :, at] = residual
            top = jnp.max(jnp.abs(residual), axis=1, keepdims=True)
            peak = top if peak is None else jnp.maximum(peak, top)
        small_ref[2 * m : 2 * m + 1] = squares[:, :128]
        small_ref[2 * m + 1 : 2 * m + 2] = squares[:, 128:]
        small_ref[4 + m : 5 + m] = turned_row(peak)


def finish(place, inv, power, summed, blocks):
    return pl.pallas_call(
        finish_body,
        in_specs=[pl.BlockSpec(memory_space=pltpu.SMEM)]
        + [pl.BlockSpec(memory_space=pltpu.VMEM)] * 10,
        out_specs=[pl.BlockSpec(memory_space=pltpu.VMEM)] * 4,
        out_shape=[
            f32(MATS, COLS, RANK),
            f32(MATS, ROWS, RANK),
            f32(MATS, ROWS, COLS),
            f32(8, 128),
        ],
        compiler_params=params(),
        cost_estimate=pl.CostEstimate(
            flops=1_300_000_000, bytes_accessed=7_000_000, transcendentals=0
        ),
        name="finish",
    )(place, inv, power, *summed, *blocks)


def outputs_body(
    place_ref, small_ref, back_ref, ortho_ref, residual_ref, weight_ref,
    momentum_ref, peaks_ref, basis_ref, new_weight_ref,
):
    total = small_ref[0]
    for i in range(1, 8):
        total = total + small_ref[i]
    block = place_ref[1]
    for m in range(MATS):
        squares = jnp.concatenate([total[2 * m : 2 * m + 1], total[2 * m + 1 : 2 * m + 2]], axis=1)
        norm = lax.rsqrt(squares + epsilon)
        basis = back_ref[m] * norm
        basis_ref[m] = basis.astype(jnp.bfloat16)
        for b in range(D // BLOCK):
            peaks_ref[m, b : b + 1] = jnp.maximum(
                small_ref[2 * b, 4 + m : 5 + m], small_ref[2 * b + 1, 4 + m : 5 + m]
            )
        mine = jnp.maximum(
            small_ref[2 * block, 4 + m : 5 + m], small_ref[2 * block + 1, 4 + m : 5 + m]
        )
        scale = turned_column(mine) + epsilon
        scale = jnp.concatenate([scale] * (COLS // 128), axis=1)
        momentum_ref[m] = (residual_ref[m] / scale).astype(jnp.bfloat16)
        update = near_dot(ortho_ref[m], basis, ((1,), (1,))) * (D / math.sqrt(RANK))
        new_weight_ref[m] = (weight_ref[m].astype(jnp.float32) - step_size * update).astype(
            jnp.bfloat16
        )


def outputs(place, small, back, ortho, residual, weight):
    return pl.pallas_call(
        outputs_body,
        in_specs=[pl.BlockSpec(memory_space=pltpu.SMEM)]
        + [pl.BlockSpec(memory_space=pltpu.VMEM)] * 5,
        out_specs=[pl.BlockSpec(memory_space=pltpu.VMEM)] * 4,
        out_shape=[
            jax.ShapeDtypeStruct((MATS, ROWS, COLS), jnp.bfloat16),
            f32(MATS, D // BLOCK, ROWS),
            jax.ShapeDtypeStruct((MATS, COLS, RANK), jnp.bfloat16),
            jax.ShapeDtypeStruct((MATS, ROWS, COLS), jnp.bfloat16),
        ],
        compiler_params=params(),
        cost_estimate=pl.CostEstimate(
            flops=500_000_000, bytes_accessed=7_000_000, transcendentals=0
        ),
        name="outputs",
    )(place, small, back, ortho, residual, weight)


ROW_AXES = ("zh", "zl", "yh", "yl")


def shift(value, z_step, y_step):
    pairs = [
        (z * 8 + y, (z + z_step) % 8 * 8 + (y + y_step) % 8) for z in range(8) for y in range(8)
    ]
    return lax.ppermute(value, ROW_AXES, pairs)


def swap(value, z_flip, y_flip):
    pairs = [(z * 8 + y, (z ^ z_flip) * 8 + (y ^ y_flip)) for z in range(8) for y in range(8)]
    return lax.ppermute(value, ROW_AXES, pairs)


def per_device(codes, scales, table, gradient, weight, basis):
    place = jnp.stack([lax.axis_index(axis) for axis in ("yl", "x", "zl", "core")])
    place = place.astype(jnp.int32)
    tables = jnp.concatenate(
        [jnp.swapaxes(scales, 1, 2).reshape(8, ROWS), table.reshape(2, 128)], axis=0
    )
    *blocks, partial_power = decode(place, codes, tables, gradient, basis)

    from_y = swap(blocks[1], 0, 1)
    from_z = swap(blocks[2], 1, 0)
    from_diagonal = swap(blocks[3], 1, 1)

    pieces = lax.all_to_all(partial_power.reshape(8, 32, RANK), COLS_AXES, 0, 0, tiled=True)
    piece = jnp.sum(pieces, axis=0)
    near = everyone(piece, GROUP)
    far = lax.ppermute(near, "core", [(0, 1), (1, 0)])

    near_rows = stack_rows(blocks[0], from_y)
    far_rows = stack_rows(from_z, from_diagonal)
    pieces, power = cross(place, (*near_rows, *far_rows), near, far)
    pieces = lax.all_to_all(pieces, OTHERS, 0, 0, tiled=True)
    piece = jnp.sum(pieces, axis=0)
    own = everyone(piece, OTHERS)
    y = shift(own, 0, 1)
    z = shift(own, 1, 0)
    diagonal = shift(own, -1, -1)
    gram = everyone(own[:, 64:].reshape(128, 128), COLS_AXES)
    inv = inverse_factor(gram)

    back, ortho, residual, small = finish(place, inv, power, (own, y, z, diagonal), blocks)
    small = everyone(small, COLS_AXES)
    new_momentum, peaks, new_basis, new_weight = outputs(
        place, small, back, ortho, residual, weight
    )
    return new_momentum, jnp.swapaxes(peaks, 1, 2), new_basis, new_weight


def solution(mesh):
    axes = ("zh", "zl", "yh", "yl", "x", "core")
    fine = Mesh(mesh.devices.reshape(4, 2, 4, 2, 4, 2), axes)
    rows = axes[:4]
    cols = axes[4:]
    return jax.shard_map(
        per_device,
        mesh=fine,
        in_specs=(
            P(None, rows, cols),
            P(None, rows, None),
            P(),
            P(None, rows, cols),
            P(None, rows, cols),
            P(None, cols, None),
        ),
        out_specs=(
            P(None, rows, cols),
            P(None, rows, None),
            P(None, cols, None),
            P(None, rows, cols),
        ),
        check_vma=False,
    )
```

```python
import math

import jax
import jax.numpy as jnp
from jax import lax
from jax.experimental import pallas as pl
from jax.experimental.pallas import tpu as pltpu
from jax.sharding import Mesh
from jax.sharding import PartitionSpec as P


D = 8192
RANK = 256
BLOCK = 2048
MATS = 2

epsilon = 1e-06
momentum_decay = 0.95
step_size = 0.5

ROWS = 128
COLS = 1024
QUARTER = COLS // 4
PIECE = 72
BLOCKED = 64
COLS_AXES = ("x", "core")
GROUP = ("zl", "yl", "x")
OTHERS = ("zh", "yh")


def f32(*shape):
    return jax.ShapeDtypeStruct(shape, jnp.float32)


def high_dot(a, b, dims):
    return lax.dot_general(
        a, b, (dims, ((), ())), precision=lax.Precision.HIGHEST, preferred_element_type=jnp.float32
    )


def split_dot(a, b):
    total = None
    for _ in range(3):
        term = a.astype(jnp.bfloat16)
        a = a - term.astype(jnp.float32)
        part = jnp.dot(term, b, preferred_element_type=jnp.float32)
        total = part if total is None else total + part
    return total


def near_dot(a, b, dims):
    a_top = a.astype(jnp.bfloat16)
    b_top = b.astype(jnp.bfloat16)
    a_rest = (a - a_top.astype(jnp.float32)).astype(jnp.bfloat16)
    b_rest = (b - b_top.astype(jnp.float32)).astype(jnp.bfloat16)

    def dot(x, y):
        return lax.dot_general(x, y, (dims, ((), ())), preferred_element_type=jnp.float32)

    return dot(a_top, b_top) + (dot(a_top, b_rest) + dot(a_rest, b_top))


def params():
    return pltpu.CompilerParams(vmem_limit_bytes=24 * 1024 * 1024)


def everyone(value, axes):
    count = lax.axis_size(axes)
    copies = jnp.broadcast_to(value, (count, *value.shape))
    return lax.all_to_all(copies, axes, 0, 0, tiled=True)


def quarter_of(place_ref, turn):
    y, z = place_ref[0], place_ref[2]
    return 2 * (1 - z if turn // 2 else z) + (1 - y if turn % 2 else y)


def turned_row(column):
    return jnp.transpose(jnp.broadcast_to(column, (ROWS, 128)))[0:1]


def turned_column(row):
    return jnp.transpose(jnp.broadcast_to(row, (128, ROWS)))


def decode_body(
    place_ref, codes_hbm, small_ref, grad_hbm, basis_hbm,
    own_ref, y_ref, z_ref, diagonal_ref, power_ref,
    codes_ref, grad_ref, basis_ref, sems,
):
    block = place_ref[1]
    arrays = ((codes_hbm, codes_ref), (grad_hbm, grad_ref), (basis_hbm, basis_ref))
    copies = {
        (m, i): pltpu.make_async_copy(source.at[m], target.at[m], sems.at[m, i])
        for m in range(MATS)
        for i, (source, target) in enumerate(arrays)
    }
    for m, i in ((0, 0), (0, 1), (0, 2), (1, 0), (1, 1), (1, 2)):
        copies[m, i].start()
    low = jnp.broadcast_to(small_ref[8:9], (ROWS, 128))
    high = jnp.broadcast_to(small_ref[9:10], (ROWS, 128))
    for m in range(MATS):
        copies[m, 0].wait()
        copies[m, 1].wait()
        scale = turned_column(small_ref[pl.ds(4 * m + block, 1), :])
        both = []
        for turn, out_ref in enumerate((own_ref, y_ref, z_ref, diagonal_ref)):
            start = quarter_of(place_ref, turn) * QUARTER
            pieces = []
            for t in range(QUARTER // 128):
                lanes = pl.ds(pl.multiple_of(start + t * 128, 128), 128)
                code = codes_ref[m, :, lanes]
                index = code & 127
                value = jnp.where(
                    code < 128,
                    jnp.take_along_axis(low, index, axis=1),
                    jnp.take_along_axis(high, index, axis=1),
                )
                pieces.append(value * scale + grad_ref[m, :, lanes].astype(jnp.float32))
            piece = jnp.concatenate(pieces, axis=1)
            out_ref[m] = piece
            both.append((start, piece))
        copies[m, 2].wait()
        parts = [
            split_dot(piece, basis_ref[m, pl.ds(pl.multiple_of(start, QUARTER), QUARTER), :])
            for start, piece in both
        ]
        power_ref[m] = (parts[0] + parts[1]) + (parts[2] + parts[3])


def decode(place, codes, small, gradient, basis):
    return pl.pallas_call(
        decode_body,
        in_specs=[
            pl.BlockSpec(memory_space=pltpu.SMEM),
            pl.BlockSpec(memory_space=pltpu.HBM),
            pl.BlockSpec(memory_space=pltpu.VMEM),
            pl.BlockSpec(memory_space=pltpu.HBM),
            pl.BlockSpec(memory_space=pltpu.HBM),
        ],
        out_specs=[pl.BlockSpec(memory_space=pltpu.VMEM)] * 5,
        out_shape=[f32(MATS, ROWS, QUARTER)] * 4 + [f32(MATS, ROWS, RANK)],
        scratch_shapes=[
            pltpu.VMEM(codes.shape, codes.dtype),
            pltpu.VMEM(gradient.shape, gradient.dtype),
            pltpu.VMEM(basis.shape, basis.dtype),
            pltpu.SemaphoreType.DMA((MATS, 3)),
        ],
        compiler_params=pltpu.CompilerParams(vmem_limit_bytes=53600 * 1024),
        cost_estimate=pl.CostEstimate(flops=400_000_000, bytes_accessed=4_000_000, transcendentals=0),
        name="decode",
    )(place, codes, small, gradient, basis)


def stack_rows_body(first_ref, second_ref, top_ref, rest_ref):
    for i, ref in enumerate((first_ref, second_ref)):
        for m in range(MATS):
            value = ref[m]
            top = value.astype(jnp.bfloat16)
            at = slice(ROWS * i, ROWS * i + ROWS)
            top_ref[m, at, :] = top
            rest_ref[m, at, :] = (value - top.astype(jnp.float32)).astype(jnp.bfloat16)


def stack_rows(first, second):
    return pl.pallas_call(
        stack_rows_body,
        in_specs=[pl.BlockSpec(memory_space=pltpu.VMEM)] * 2,
        out_specs=[pl.BlockSpec(memory_space=pltpu.VMEM)] * 2,
        out_shape=[jax.ShapeDtypeStruct((MATS, 2 * ROWS, QUARTER), jnp.bfloat16)] * 2,
        compiler_params=params(),
        cost_estimate=pl.CostEstimate(flops=400_000, bytes_accessed=1_000_000, transcendentals=0),
        name="stack_rows",
    )(first, second)


def cross_body(
    place_ref, near_top_ref, near_rest_ref, far_top_ref, far_rest_ref, near_ref, far_ref,
    pieces_ref, own_power_ref, power_ref,
):
    block, core = place_ref[1], place_ref[3]
    for neighbour in range(4):
        for x in range(4):
            power_ref[neighbour, 2 * x + core] = near_ref[4 * neighbour + x]
            power_ref[neighbour, 2 * x + 1 - core] = far_ref[4 * neighbour + x]
    neighbours = [quarter_of(place_ref, turn) for turn in range(4)]
    for m in range(MATS):
        rows = [power_ref[n, 4 * m : 4 * m + 4].reshape(ROWS, RANK) for n in neighbours]
        own_power_ref[m] = rows[0]
        right = jnp.concatenate(rows, axis=0)
        right_top = right.astype(jnp.bfloat16)
        right_rest = (right - right_top.astype(jnp.float32)).astype(jnp.bfloat16)
        top = jnp.concatenate([near_top_ref[m], far_top_ref[m]], axis=0)
        rest = jnp.concatenate([near_rest_ref[m], far_rest_ref[m]], axis=0)
        product = low_dot(top, right_top) + (low_dot(top, right_rest) + low_dot(rest, right_top))
        for h in range(2):
            pieces_ref[8 * m : 8 * m + 8, 32 * h : 32 * h + 32, :] = product[
                :, 128 * h : 128 * h + 128
            ].reshape(8, 32, 128)
    mat = pl.ds(block // 2 * 4, 4)
    sides = []
    for part in (block % 2, core):
        lanes = pl.ds(pl.multiple_of(part * 128, 128), 128)
        sides.append(
            jnp.concatenate(
                [power_ref[n, mat, :, lanes].reshape(ROWS, 128) for n in range(4)], axis=0
            )
        )
    pieces_ref[:, 64:72, :] = high_dot(sides[0], sides[1], ((0,), (0,))).reshape(16, 8, 128)


def low_dot(a, b):
    return lax.dot_general(a, b, (((0,), (0,)), ((), ())), preferred_element_type=jnp.float32)


def cross(place, stacked, near, far):
    return pl.pallas_call(
        cross_body,
        in_specs=[pl.BlockSpec(memory_space=pltpu.SMEM)]
        + [pl.BlockSpec(memory_space=pltpu.VMEM)] * 6,
        out_specs=[pl.BlockSpec(memory_space=pltpu.VMEM)] * 2,
        out_shape=[f32(16, PIECE, 128), f32(MATS, ROWS, RANK)],
        scratch_shapes=[pltpu.VMEM((4, 8, 32, RANK), jnp.float32)],
        compiler_params=params(),
        cost_estimate=pl.CostEstimate(flops=800_000_000, bytes_accessed=2_600_000, transcendentals=0),
        name="cross",
    )(place, *stacked, near, far)


def part_body(own_ref, plain_ref, gram_ref):
    plain_ref[...] = own_ref[:, :64]
    gram = own_ref[:, 64:].reshape(128, 128)
    for i in range(8):
        gram_ref[i] = gram


def part(own):
    return pl.pallas_call(
        part_body,
        in_specs=[pl.BlockSpec(memory_space=pltpu.VMEM)],
        out_specs=[pl.BlockSpec(memory_space=pltpu.VMEM)] * 2,
        out_shape=[f32(16, 64, 128), f32(8, 128, 128)],
        compiler_params=params(),
        cost_estimate=pl.CostEstimate(flops=1, bytes_accessed=1_600_000, transcendentals=0),
        name="part",
    )(own)


def lane_copy(tile, lane):
    return jnp.take_along_axis(tile, jnp.full((8, 128), lane, jnp.int32), axis=1)


def row_copy(tile, row):
    return jnp.broadcast_to(tile[row : row + 1], (8, 128))


def eliminate(tiles, base):
    sub = lax.broadcasted_iota(jnp.int32, (8, 128), 0)
    tiles = list(tiles)
    done = []
    for t in range(8):
        at = base + 8 * t
        work = [lane_copy(tiles[t], at + i) for i in range(8)] + [tiles[t]]
        steps = []
        rows = [None] * 8
        for p in range(0, 8, 2):
            a = row_copy(work[p], p)
            b = row_copy(work[p + 1], p)
            c = row_copy(work[p + 1], p + 1)
            det = a * c - b * b
            inv_det = 1.0 / det
            ca, cb, cc = a * inv_det, b * inv_det, c * inv_det
            later = sub > p + 1
            left = jnp.where(later, work[p], 0.0)
            right = jnp.where(later, work[p + 1], 0.0)
            step = {}
            for i in range(p + 2, 9):
                x = row_copy(work[i], p)
                y = row_copy(work[i], p + 1)
                step[i] = (cc * x - cb * y, ca * y - cb * x)
                if i == 8:
                    rows[p] = x * lax.rsqrt(a)
                    rows[p + 1] = (y - (b / a) * x) * lax.rsqrt(det / a)
                work[i] = work[i] - (left * step[i][0] + right * step[i][1])
            steps.append(step)
        out = rows[0]
        for p in range(1, 8):
            out = jnp.where(sub == p, rows[p], out)
        done.append(out)
        for u in range(t + 1, 8):
            work = [lane_copy(tiles[u], at + i) for i in range(8)] + [tiles[u]]
            for p in range(0, 8, 2):
                step = steps[p // 2]
                for i in range(p + 2, 9):
                    work[i] = work[i] - (work[p] * step[i][0] + work[p + 1] * step[i][1])
            tiles[u] = work[8]
    return jnp.concatenate(done, axis=0)


def factor_body(gram_ref, inv_ref, state_ref):
    n = BLOCKED
    lane = lax.broadcasted_iota(jnp.int32, (n, 128), 1)
    sub = lax.broadcasted_iota(jnp.int32, (n, 128), 0)
    wide = lax.broadcasted_iota(jnp.int32, (n, RANK), 1)
    deep = lax.broadcasted_iota(jnp.int32, (n, RANK), 0)
    for m in range(MATS):
        for top in range(2):
            for h in range(2):
                state_ref[m, 128 * top : 128 * top + 128, 128 * h : 128 * h + 128] = gram_ref[
                    4 * m + 2 * top + h
                ]
    for k in range(RANK // n):
        at = k * n
        base = at % 128
        mine = (lane >= base) & (lane < base + n)
        eye = (jnp.where(lane < n, lane, lane - n) == sub).astype(jnp.float32)
        reduced = []
        for m in range(MATS):
            pair = state_ref[m, at : at + n, at - base : at - base + 128]
            block = jnp.where(mine, pair, eye)
            reduced.append(eliminate([block[8 * t : 8 * t + 8] for t in range(8)], base))
        for m in range(MATS):
            low_inv = jnp.where(mine, 0.0, reduced[m])
            rows = jnp.where(
                (wide >= at) & (wide < at + n),
                (wide - at == deep).astype(jnp.float32),
                state_ref[m, at : at + n, :],
            )
            fresh = high_dot(low_inv, jnp.concatenate([rows, rows], axis=0), ((1,), (0,)))
            inv_ref[m, at : at + n, :] = jnp.where(wide < at + n, fresh, 0.0)
            if k == RANK // n - 1:
                continue
            start = (at + n) // 128 * 128
            upper = jnp.where(wide >= at + n, fresh, 0.0)[:, start:]
            change = high_dot(upper, fresh, ((0,), (0,)))
            for r in range(at + n, RANK, n):
                old = state_ref[m, r : r + n, :]
                old = jnp.where((wide >= at) & (wide < at + n), 0.0, old)
                state_ref[m, r : r + n, :] = old - change[r - start : r - start + n]


def inverse_factor(gram):
    return pl.pallas_call(
        factor_body,
        in_specs=[pl.BlockSpec(memory_space=pltpu.VMEM)],
        out_specs=pl.BlockSpec(memory_space=pltpu.VMEM),
        out_shape=f32(MATS, RANK, RANK),
        scratch_shapes=[pltpu.VMEM((MATS, RANK, RANK), jnp.float32)],
        compiler_params=params(),
        cost_estimate=pl.CostEstimate(
            flops=4_000_000_000, bytes_accessed=1_000_000, transcendentals=0
        ),
        name="inverse_factor",
    )(gram)


def finish_body(
    place_ref, inv_ref, power_ref, own_ref, y_ref, z_ref, diagonal_ref,
    own_buffer_ref, y_buffer_ref, z_buffer_ref, diagonal_buffer_ref,
    back_ref, ortho_ref, residual_ref, small_ref,
):
    summed_refs = (own_ref, y_ref, z_ref, diagonal_ref)
    buffer_refs = (own_buffer_ref, y_buffer_ref, z_buffer_ref, diagonal_buffer_ref)
    small_ref[6:8] = jnp.zeros((2, 128), jnp.float32)
    for m in range(MATS):
        factor = inv_ref[m]
        ortho = high_dot(power_ref[m], factor, ((1,), (1,)))
        ortho_ref[m] = ortho
        squares = None
        peak = None
        for turn in range(4):
            pieces = summed_refs[turn][8 * m : 8 * m + 8]
            summed = jnp.concatenate(
                [pieces[:, :32].reshape(QUARTER, 128), pieces[:, 32:64].reshape(QUARTER, 128)],
                axis=1,
            )
            back = near_dot(summed, factor, ((1,), (1,)))
            at = pl.ds(pl.multiple_of(quarter_of(place_ref, turn) * QUARTER, QUARTER), QUARTER)
            back_ref[m, at, :] = back
            part = jnp.sum(back * back, axis=0, keepdims=True)
            squares = part if squares is None else squares + part
            residual = buffer_refs[turn][m] - (1.0 - momentum_decay) * near_dot(
                ortho, back, ((1,), (1,))
            )
            residual_ref[m, :, at] = residual
            top = jnp.max(jnp.abs(residual), axis=1, keepdims=True)
            peak = top if peak is None else jnp.maximum(peak, top)
        small_ref[2 * m : 2 * m + 1] = squares[:, :128]
        small_ref[2 * m + 1 : 2 * m + 2] = squares[:, 128:]
        small_ref[4 + m : 5 + m] = turned_row(peak)


def finish(place, inv, power, summed, blocks):
    return pl.pallas_call(
        finish_body,
        in_specs=[pl.BlockSpec(memory_space=pltpu.SMEM)]
        + [pl.BlockSpec(memory_space=pltpu.VMEM)] * 10,
        out_specs=[pl.BlockSpec(memory_space=pltpu.VMEM)] * 4,
        out_shape=[
            f32(MATS, COLS, RANK),
            f32(MATS, ROWS, RANK),
            f32(MATS, ROWS, COLS),
            f32(8, 128),
        ],
        compiler_params=params(),
        cost_estimate=pl.CostEstimate(
            flops=1_300_000_000, bytes_accessed=7_000_000, transcendentals=0
        ),
        name="finish",
    )(place, inv, power, *summed, *blocks)


def outputs_body(
    place_ref, small_ref, back_ref, ortho_ref, residual_ref, weight_ref,
    momentum_hbm, peaks_ref, basis_hbm, new_weight_hbm,
    momentum_ref, basis_ref, new_weight_ref, sems,
):
    total = small_ref[0]
    for i in range(1, 8):
        total = total + small_ref[i]
    block = place_ref[1]
    copies = []

    def send(m, i, source, target):
        copies.append(pltpu.make_async_copy(source.at[m], target.at[m], sems.at[m, i]))
        copies[-1].start()

    for m in range(MATS):
        squares = jnp.concatenate([total[2 * m : 2 * m + 1], total[2 * m + 1 : 2 * m + 2]], axis=1)
        norm = lax.rsqrt(squares + epsilon)
        basis_ref[m] = (back_ref[m] * norm).astype(jnp.bfloat16)
        send(m, 0, basis_ref, basis_hbm)
        for b in range(D // BLOCK):
            peaks_ref[m, b : b + 1] = jnp.maximum(
                small_ref[2 * b, 4 + m : 5 + m], small_ref[2 * b + 1, 4 + m : 5 + m]
            )
        mine = jnp.maximum(
            small_ref[2 * block, 4 + m : 5 + m], small_ref[2 * block + 1, 4 + m : 5 + m]
        )
        scale = turned_column(mine) + epsilon
        scale = jnp.concatenate([scale] * (COLS // 128), axis=1)
        momentum_ref[m] = (residual_ref[m] / scale).astype(jnp.bfloat16)
        send(m, 1, momentum_ref, momentum_hbm)
        left = ortho_ref[m] * (norm * (step_size * D / math.sqrt(RANK)))
        update = near_dot(left, back_ref[m], ((1,), (1,)))
        new_weight_ref[m] = (weight_ref[m].astype(jnp.float32) - update).astype(jnp.bfloat16)
        send(m, 2, new_weight_ref, new_weight_hbm)
    for copy in copies:
        copy.wait()


def outputs(place, small, back, ortho, residual, weight):
    rows_shape = (MATS, ROWS, COLS)
    basis_shape = (MATS, COLS, RANK)
    hbm = pl.BlockSpec(memory_space=pltpu.HBM)
    return pl.pallas_call(
        outputs_body,
        in_specs=[pl.BlockSpec(memory_space=pltpu.SMEM)]
        + [pl.BlockSpec(memory_space=pltpu.VMEM)] * 5,
        out_specs=[hbm, pl.BlockSpec(memory_space=pltpu.VMEM), hbm, hbm],
        out_shape=[
            jax.ShapeDtypeStruct(rows_shape, jnp.bfloat16),
            f32(MATS, D // BLOCK, ROWS),
            jax.ShapeDtypeStruct(basis_shape, jnp.bfloat16),
            jax.ShapeDtypeStruct(rows_shape, jnp.bfloat16),
        ],
        scratch_shapes=[
            pltpu.VMEM(rows_shape, jnp.bfloat16),
            pltpu.VMEM(basis_shape, jnp.bfloat16),
            pltpu.VMEM(rows_shape, jnp.bfloat16),
            pltpu.SemaphoreType.DMA((MATS, 3)),
        ],
        compiler_params=params(),
        cost_estimate=pl.CostEstimate(
            flops=500_000_000, bytes_accessed=7_000_000, transcendentals=0
        ),
        name="outputs",
    )(place, small, back, ortho, residual, weight)


ROW_AXES = ("zh", "zl", "yh", "yl")


def shift(value, z_step, y_step):
    pairs = [
        (z * 8 + y, (z + z_step) % 8 * 8 + (y + y_step) % 8) for z in range(8) for y in range(8)
    ]
    return lax.ppermute(value, ROW_AXES, pairs)


def swap(value, z_flip, y_flip):
    pairs = [(z * 8 + y, (z ^ z_flip) * 8 + (y ^ y_flip)) for z in range(8) for y in range(8)]
    return lax.ppermute(value, ROW_AXES, pairs)


def per_device(codes, scales, table, gradient, weight, basis):
    place = jnp.stack([lax.axis_index(axis) for axis in ("yl", "x", "zl", "core")])
    place = place.astype(jnp.int32)
    tables = jnp.concatenate(
        [jnp.swapaxes(scales, 1, 2).reshape(8, ROWS), table.reshape(2, 128)], axis=0
    )
    *blocks, partial_power = decode(place, codes, tables, gradient, basis)

    from_y = swap(blocks[1], 0, 1)
    from_z = swap(blocks[2], 1, 0)
    from_diagonal = swap(blocks[3], 1, 1)

    pieces = lax.all_to_all(partial_power.reshape(8, 32, RANK), COLS_AXES, 0, 0, tiled=True)
    piece = jnp.sum(pieces, axis=0)
    near = everyone(piece, GROUP)
    far = lax.ppermute(near, "core", [(0, 1), (1, 0)])

    near_rows = stack_rows(blocks[0], from_y)
    far_rows = stack_rows(from_z, from_diagonal)
    pieces, power = cross(place, (*near_rows, *far_rows), near, far)
    pieces = lax.all_to_all(pieces, OTHERS, 0, 0, tiled=True)
    piece = jnp.sum(pieces, axis=0)
    own = everyone(piece, OTHERS)
    plain, gram = part(own)
    y = shift(plain, 0, 1)
    z = shift(plain, 1, 0)
    diagonal = shift(plain, -1, -1)
    gram = lax.all_to_all(gram, COLS_AXES, 0, 0, tiled=True)
    inv = inverse_factor(gram)

    back, ortho, residual, small = finish(place, inv, power, (plain, y, z, diagonal), blocks)
    small = everyone(small, COLS_AXES)
    new_momentum, peaks, new_basis, new_weight = outputs(
        place, small, back, ortho, residual, weight
    )
    return new_momentum, jnp.swapaxes(peaks, 1, 2), new_basis, new_weight


def solution(mesh):
    axes = ("zh", "zl", "yh", "yl", "x", "core")
    fine = Mesh(mesh.devices.reshape(4, 2, 4, 2, 4, 2), axes)
    rows = axes[:4]
    cols = axes[4:]
    return jax.shard_map(
        per_device,
        mesh=fine,
        in_specs=(
            P(None, rows, cols),
            P(None, rows, None),
            P(),
            P(None, rows, cols),
            P(None, rows, cols),
            P(None, cols, None),
        ),
        out_specs=(
            P(None, rows, cols),
            P(None, rows, None),
            P(None, cols, None),
            P(None, rows, cols),
        ),
        check_vma=False,
    )
```

```python
import math

import jax
import jax.numpy as jnp
from jax import lax
from jax.experimental import pallas as pl
from jax.experimental.pallas import tpu as pltpu
from jax.sharding import Mesh
from jax.sharding import PartitionSpec as P


D = 8192
RANK = 256
BLOCK = 2048
MATS = 2

epsilon = 1e-06
momentum_decay = 0.95
step_size = 0.5

ROWS = 128
COLS = 1024
QUARTER = COLS // 4
PIECE = 72
BLOCKED = 64
COLS_AXES = ("x", "core")
GROUP = ("zl", "yl", "x")
OTHERS = ("zh", "yh")


def f32(*shape):
    return jax.ShapeDtypeStruct(shape, jnp.float32)


def high_dot(a, b, dims):
    return lax.dot_general(
        a, b, (dims, ((), ())), precision=lax.Precision.HIGHEST, preferred_element_type=jnp.float32
    )


def split_dot(a, b):
    total = None
    for _ in range(3):
        term = a.astype(jnp.bfloat16)
        a = a - term.astype(jnp.float32)
        part = jnp.dot(term, b, preferred_element_type=jnp.float32)
        total = part if total is None else total + part
    return total


def near_dot(a, b, dims):
    a_top = a.astype(jnp.bfloat16)
    b_top = b.astype(jnp.bfloat16)
    a_rest = (a - a_top.astype(jnp.float32)).astype(jnp.bfloat16)
    b_rest = (b - b_top.astype(jnp.float32)).astype(jnp.bfloat16)

    def dot(x, y):
        return lax.dot_general(x, y, (dims, ((), ())), preferred_element_type=jnp.float32)

    return dot(a_top, b_top) + (dot(a_top, b_rest) + dot(a_rest, b_top))


def split_pair_dot(a, b_top, b_rest):
    a_top = a.astype(jnp.bfloat16)
    a_rest = (a - a_top.astype(jnp.float32)).astype(jnp.bfloat16)

    def dot(x, y):
        return lax.dot_general(x, y, (((1,), (1,)), ((), ())), preferred_element_type=jnp.float32)

    return dot(a_top, b_top) + (dot(a_top, b_rest) + dot(a_rest, b_top))


def params():
    return pltpu.CompilerParams(vmem_limit_bytes=24 * 1024 * 1024)


def everyone(value, axes):
    count = lax.axis_size(axes)
    copies = jnp.broadcast_to(value, (count, *value.shape))
    return lax.all_to_all(copies, axes, 0, 0, tiled=True)


def quarter_of(place_ref, turn):
    y, z = place_ref[0], place_ref[2]
    return 2 * (1 - z if turn // 2 else z) + (1 - y if turn % 2 else y)


def turned_row(column):
    return jnp.transpose(jnp.broadcast_to(column, (ROWS, 128)))[0:1]


def turned_column(row):
    return jnp.transpose(jnp.broadcast_to(row, (128, ROWS)))


def decode_body(
    place_ref, codes_hbm, small_ref, grad_hbm, basis_hbm,
    own_ref, y_ref, z_ref, diagonal_ref, power_ref,
    codes_ref, grad_ref, basis_ref, sems,
):
    block = place_ref[1]
    arrays = ((codes_hbm, codes_ref), (grad_hbm, grad_ref), (basis_hbm, basis_ref))
    copies = {
        (m, i): pltpu.make_async_copy(source.at[m], target.at[m], sems.at[m, i])
        for m in range(MATS)
        for i, (source, target) in enumerate(arrays)
    }
    for m, i in ((0, 0), (0, 1), (0, 2), (1, 0), (1, 1), (1, 2)):
        copies[m, i].start()
    low = jnp.broadcast_to(small_ref[8:9], (ROWS, 128))
    high = jnp.broadcast_to(small_ref[9:10], (ROWS, 128))
    for m in range(MATS):
        copies[m, 0].wait()
        copies[m, 1].wait()
        scale = turned_column(small_ref[pl.ds(4 * m + block, 1), :])
        both = []
        for turn, out_ref in enumerate((own_ref, y_ref, z_ref, diagonal_ref)):
            start = quarter_of(place_ref, turn) * QUARTER
            pieces = []
            for t in range(QUARTER // 128):
                lanes = pl.ds(pl.multiple_of(start + t * 128, 128), 128)
                code = codes_ref[m, :, lanes]
                index = code & 127
                value = jnp.where(
                    code < 128,
                    jnp.take_along_axis(low, index, axis=1),
                    jnp.take_along_axis(high, index, axis=1),
                )
                pieces.append(value * scale + grad_ref[m, :, lanes].astype(jnp.float32))
            piece = jnp.concatenate(pieces, axis=1)
            out_ref[m] = piece
            both.append((start, piece))
        copies[m, 2].wait()
        parts = [
            split_dot(piece, basis_ref[m, pl.ds(pl.multiple_of(start, QUARTER), QUARTER), :])
            for start, piece in both
        ]
        power_ref[m] = (parts[0] + parts[1]) + (parts[2] + parts[3])


def decode(place, codes, small, gradient, basis):
    return pl.pallas_call(
        decode_body,
        in_specs=[
            pl.BlockSpec(memory_space=pltpu.SMEM),
            pl.BlockSpec(memory_space=pltpu.HBM),
            pl.BlockSpec(memory_space=pltpu.VMEM),
            pl.BlockSpec(memory_space=pltpu.HBM),
            pl.BlockSpec(memory_space=pltpu.HBM),
        ],
        out_specs=[pl.BlockSpec(memory_space=pltpu.VMEM)] * 5,
        out_shape=[f32(MATS, ROWS, QUARTER)] * 4 + [f32(MATS, ROWS, RANK)],
        scratch_shapes=[
            pltpu.VMEM(codes.shape, codes.dtype),
            pltpu.VMEM(gradient.shape, gradient.dtype),
            pltpu.VMEM(basis.shape, basis.dtype),
            pltpu.SemaphoreType.DMA((MATS, 3)),
        ],
        compiler_params=pltpu.CompilerParams(vmem_limit_bytes=53600 * 1024),
        cost_estimate=pl.CostEstimate(flops=400_000_000, bytes_accessed=4_000_000, transcendentals=0),
        name="decode",
    )(place, codes, small, gradient, basis)


def stack_rows_body(first_ref, second_ref, top_ref, rest_ref):
    for i, ref in enumerate((first_ref, second_ref)):
        for m in range(MATS):
            value = ref[m]
            top = value.astype(jnp.bfloat16)
            at = slice(ROWS * i, ROWS * i + ROWS)
            top_ref[m, at, :] = top
            rest_ref[m, at, :] = (value - top.astype(jnp.float32)).astype(jnp.bfloat16)


def stack_rows(first, second):
    return pl.pallas_call(
        stack_rows_body,
        in_specs=[pl.BlockSpec(memory_space=pltpu.VMEM)] * 2,
        out_specs=[pl.BlockSpec(memory_space=pltpu.VMEM)] * 2,
        out_shape=[jax.ShapeDtypeStruct((MATS, 2 * ROWS, QUARTER), jnp.bfloat16)] * 2,
        compiler_params=params(),
        cost_estimate=pl.CostEstimate(flops=400_000, bytes_accessed=1_000_000, transcendentals=0),
        name="stack_rows",
    )(first, second)


def cross_body(
    place_ref, near_top_ref, near_rest_ref, far_top_ref, far_rest_ref, near_ref, far_ref,
    pieces_ref, own_power_ref, power_ref,
):
    block, core = place_ref[1], place_ref[3]
    for neighbour in range(4):
        for x in range(4):
            power_ref[neighbour, 2 * x + core] = near_ref[4 * neighbour + x]
            power_ref[neighbour, 2 * x + 1 - core] = far_ref[4 * neighbour + x]
    neighbours = [quarter_of(place_ref, turn) for turn in range(4)]
    for m in range(MATS):
        rows = [power_ref[n, 4 * m : 4 * m + 4].reshape(ROWS, RANK) for n in neighbours]
        own_power_ref[m] = rows[0]
        right = jnp.concatenate(rows, axis=0)
        right_top = right.astype(jnp.bfloat16)
        right_rest = (right - right_top.astype(jnp.float32)).astype(jnp.bfloat16)
        top = jnp.concatenate([near_top_ref[m], far_top_ref[m]], axis=0)
        rest = jnp.concatenate([near_rest_ref[m], far_rest_ref[m]], axis=0)
        product = low_dot(top, right_top) + (low_dot(top, right_rest) + low_dot(rest, right_top))
        for h in range(2):
            pieces_ref[8 * m : 8 * m + 8, 32 * h : 32 * h + 32, :] = product[
                :, 128 * h : 128 * h + 128
            ].reshape(8, 32, 128)
    mat = pl.ds(block // 2 * 4, 4)
    sides = []
    for part in (block % 2, core):
        lanes = pl.ds(pl.multiple_of(part * 128, 128), 128)
        sides.append(
            jnp.concatenate(
                [power_ref[n, mat, :, lanes].reshape(ROWS, 128) for n in range(4)], axis=0
            )
        )
    pieces_ref[:, 64:72, :] = high_dot(sides[0], sides[1], ((0,), (0,))).reshape(16, 8, 128)


def low_dot(a, b):
    return lax.dot_general(a, b, (((0,), (0,)), ((), ())), preferred_element_type=jnp.float32)


def cross(place, stacked, near, far):
    return pl.pallas_call(
        cross_body,
        in_specs=[pl.BlockSpec(memory_space=pltpu.SMEM)]
        + [pl.BlockSpec(memory_space=pltpu.VMEM)] * 6,
        out_specs=[pl.BlockSpec(memory_space=pltpu.VMEM)] * 2,
        out_shape=[f32(16, PIECE, 128), f32(MATS, ROWS, RANK)],
        scratch_shapes=[pltpu.VMEM((4, 8, 32, RANK), jnp.float32)],
        compiler_params=params(),
        cost_estimate=pl.CostEstimate(flops=800_000_000, bytes_accessed=2_600_000, transcendentals=0),
        name="cross",
    )(place, *stacked, near, far)


def part_body(own_ref, plain_ref, gram_ref):
    plain_ref[...] = own_ref[:, :64]
    gram = own_ref[:, 64:].reshape(128, 128)
    for i in range(8):
        gram_ref[i] = gram


def part(own):
    return pl.pallas_call(
        part_body,
        in_specs=[pl.BlockSpec(memory_space=pltpu.VMEM)],
        out_specs=[pl.BlockSpec(memory_space=pltpu.VMEM)] * 2,
        out_shape=[f32(16, 64, 128), f32(8, 128, 128)],
        compiler_params=params(),
        cost_estimate=pl.CostEstimate(flops=1, bytes_accessed=1_600_000, transcendentals=0),
        name="part",
    )(own)


def lane_copy(tile, lane):
    return jnp.take_along_axis(tile, jnp.full((8, 128), lane, jnp.int32), axis=1)


def row_copy(tile, row):
    return jnp.broadcast_to(tile[row : row + 1], (8, 128))


def eliminate(tiles, base):
    sub = lax.broadcasted_iota(jnp.int32, (8, 128), 0)
    tiles = list(tiles)
    done = []
    for t in range(8):
        at = base + 8 * t
        work = [lane_copy(tiles[t], at + i) for i in range(8)] + [tiles[t]]
        steps = []
        rows = [None] * 8
        for p in range(0, 8, 2):
            a = row_copy(work[p], p)
            b = row_copy(work[p + 1], p)
            c = row_copy(work[p + 1], p + 1)
            det = a * c - b * b
            inv_det = 1.0 / det
            ca, cb, cc = a * inv_det, b * inv_det, c * inv_det
            later = sub > p + 1
            left = jnp.where(later, work[p], 0.0)
            right = jnp.where(later, work[p + 1], 0.0)
            step = {}
            for i in range(p + 2, 9):
                x = row_copy(work[i], p)
                y = row_copy(work[i], p + 1)
                step[i] = (cc * x - cb * y, ca * y - cb * x)
                if i == 8:
                    rows[p] = x * lax.rsqrt(a)
                    rows[p + 1] = (y - (b / a) * x) * lax.rsqrt(det / a)
                work[i] = work[i] - (left * step[i][0] + right * step[i][1])
            steps.append(step)
        out = rows[0]
        for p in range(1, 8):
            out = jnp.where(sub == p, rows[p], out)
        done.append(out)
        for u in range(t + 1, 8):
            work = [lane_copy(tiles[u], at + i) for i in range(8)] + [tiles[u]]
            for p in range(0, 8, 2):
                step = steps[p // 2]
                for i in range(p + 2, 9):
                    work[i] = work[i] - (work[p] * step[i][0] + work[p + 1] * step[i][1])
            tiles[u] = work[8]
    return jnp.concatenate(done, axis=0)


def factor_body(gram_ref, inv_ref, state_ref):
    n = BLOCKED
    lane = lax.broadcasted_iota(jnp.int32, (n, 128), 1)
    sub = lax.broadcasted_iota(jnp.int32, (n, 128), 0)
    wide = lax.broadcasted_iota(jnp.int32, (n, RANK), 1)
    deep = lax.broadcasted_iota(jnp.int32, (n, RANK), 0)
    for m in range(MATS):
        for top in range(2):
            for h in range(2):
                state_ref[m, 128 * top : 128 * top + 128, 128 * h : 128 * h + 128] = gram_ref[
                    4 * m + 2 * top + h
                ]
    for k in range(RANK // n):
        at = k * n
        base = at % 128
        mine = (lane >= base) & (lane < base + n)
        eye = (jnp.where(lane < n, lane, lane - n) == sub).astype(jnp.float32)
        reduced = []
        for m in range(MATS):
            pair = state_ref[m, at : at + n, at - base : at - base + 128]
            block = jnp.where(mine, pair, eye)
            reduced.append(eliminate([block[8 * t : 8 * t + 8] for t in range(8)], base))
        for m in range(MATS):
            low_inv = jnp.where(mine, 0.0, reduced[m])
            rows = jnp.where(
                (wide >= at) & (wide < at + n),
                (wide - at == deep).astype(jnp.float32),
                state_ref[m, at : at + n, :],
            )
            fresh = high_dot(low_inv, jnp.concatenate([rows, rows], axis=0), ((1,), (0,)))
            inv_ref[m, at : at + n, :] = jnp.where(wide < at + n, fresh, 0.0)
            if k == RANK // n - 1:
                continue
            start = (at + n) // 128 * 128
            upper = jnp.where(wide >= at + n, fresh, 0.0)[:, start:]
            change = high_dot(upper, fresh, ((0,), (0,)))
            for r in range(at + n, RANK, n):
                old = state_ref[m, r : r + n, :]
                old = jnp.where((wide >= at) & (wide < at + n), 0.0, old)
                state_ref[m, r : r + n, :] = old - change[r - start : r - start + n]


def inverse_factor(gram):
    return pl.pallas_call(
        factor_body,
        in_specs=[pl.BlockSpec(memory_space=pltpu.VMEM)],
        out_specs=pl.BlockSpec(memory_space=pltpu.VMEM),
        out_shape=f32(MATS, RANK, RANK),
        scratch_shapes=[pltpu.VMEM((MATS, RANK, RANK), jnp.float32)],
        compiler_params=params(),
        cost_estimate=pl.CostEstimate(
            flops=4_000_000_000, bytes_accessed=1_000_000, transcendentals=0
        ),
        name="inverse_factor",
    )(gram)


def finish_body(
    place_ref, inv_ref, power_ref, own_ref, y_ref, z_ref, diagonal_ref,
    own_buffer_ref, y_buffer_ref, z_buffer_ref, diagonal_buffer_ref,
    top_ref, rest_ref, ortho_ref, residual_ref, small_ref,
):
    summed_refs = (own_ref, y_ref, z_ref, diagonal_ref)
    buffer_refs = (own_buffer_ref, y_buffer_ref, z_buffer_ref, diagonal_buffer_ref)
    small_ref[6:8] = jnp.zeros((2, 128), jnp.float32)
    for m in range(MATS):
        factor = inv_ref[m]
        ortho = high_dot(power_ref[m], factor, ((1,), (1,)))
        ortho_ref[m] = ortho
        squares = None
        peak = None
        for turn in range(4):
            pieces = summed_refs[turn][8 * m : 8 * m + 8]
            summed = jnp.concatenate(
                [pieces[:, :32].reshape(QUARTER, 128), pieces[:, 32:64].reshape(QUARTER, 128)],
                axis=1,
            )
            back = near_dot(summed, factor, ((1,), (1,)))
            at = pl.ds(pl.multiple_of(quarter_of(place_ref, turn) * QUARTER, QUARTER), QUARTER)
            back_top = back.astype(jnp.bfloat16)
            back_rest = (back - back_top.astype(jnp.float32)).astype(jnp.bfloat16)
            top_ref[m, at, :] = back_top
            rest_ref[m, at, :] = back_rest
            part = jnp.sum(back * back, axis=0, keepdims=True)
            squares = part if squares is None else squares + part
            residual = buffer_refs[turn][m] - (1.0 - momentum_decay) * split_pair_dot(
                ortho, back_top, back_rest
            )
            residual_ref[m, :, at] = residual
            top = jnp.max(jnp.abs(residual), axis=1, keepdims=True)
            peak = top if peak is None else jnp.maximum(peak, top)
        small_ref[2 * m : 2 * m + 1] = squares[:, :128]
        small_ref[2 * m + 1 : 2 * m + 2] = squares[:, 128:]
        small_ref[4 + m : 5 + m] = turned_row(peak)


def finish(place, inv, power, summed, blocks):
    return pl.pallas_call(
        finish_body,
        in_specs=[pl.BlockSpec(memory_space=pltpu.SMEM)]
        + [pl.BlockSpec(memory_space=pltpu.VMEM)] * 10,
        out_specs=[pl.BlockSpec(memory_space=pltpu.VMEM)] * 5,
        out_shape=[
            jax.ShapeDtypeStruct((MATS, COLS, RANK), jnp.bfloat16),
            jax.ShapeDtypeStruct((MATS, COLS, RANK), jnp.bfloat16),
            f32(MATS, ROWS, RANK),
            f32(MATS, ROWS, COLS),
            f32(8, 128),
        ],
        compiler_params=params(),
        cost_estimate=pl.CostEstimate(
            flops=1_300_000_000, bytes_accessed=7_000_000, transcendentals=0
        ),
        name="finish",
    )(place, inv, power, *summed, *blocks)


def outputs_body(
    place_ref, small_ref, top_ref, rest_ref, ortho_ref, residual_ref, weight_ref,
    momentum_ref, peaks_ref, basis_ref, new_weight_ref,
):
    total = small_ref[0]
    for i in range(1, 8):
        total = total + small_ref[i]
    block = place_ref[1]
    for m in range(MATS):
        squares = jnp.concatenate([total[2 * m : 2 * m + 1], total[2 * m + 1 : 2 * m + 2]], axis=1)
        norm = lax.rsqrt(squares + epsilon)
        top, rest = top_ref[m], rest_ref[m]
        back = top.astype(jnp.float32) + rest.astype(jnp.float32)
        basis_ref[m] = (back * norm).astype(jnp.bfloat16)
        for b in range(D // BLOCK):
            peaks_ref[m, b : b + 1] = jnp.maximum(
                small_ref[2 * b, 4 + m : 5 + m], small_ref[2 * b + 1, 4 + m : 5 + m]
            )
        mine = jnp.maximum(
            small_ref[2 * block, 4 + m : 5 + m], small_ref[2 * block + 1, 4 + m : 5 + m]
        )
        scale = 1.0 / (turned_column(mine) + epsilon)
        scale = jnp.concatenate([scale] * (COLS // 128), axis=1)
        momentum_ref[m] = (residual_ref[m] * scale).astype(jnp.bfloat16)
        left = ortho_ref[m] * (norm * (step_size * D / math.sqrt(RANK)))
        update = split_pair_dot(left, top, rest)
        new_weight_ref[m] = (weight_ref[m].astype(jnp.float32) - update).astype(jnp.bfloat16)


def outputs(place, small, top, rest, ortho, residual, weight):
    return pl.pallas_call(
        outputs_body,
        in_specs=[pl.BlockSpec(memory_space=pltpu.SMEM)]
        + [pl.BlockSpec(memory_space=pltpu.VMEM)] * 6,
        out_specs=[pl.BlockSpec(memory_space=pltpu.VMEM)] * 4,
        out_shape=[
            jax.ShapeDtypeStruct((MATS, ROWS, COLS), jnp.bfloat16),
            f32(MATS, D // BLOCK, ROWS),
            jax.ShapeDtypeStruct((MATS, COLS, RANK), jnp.bfloat16),
            jax.ShapeDtypeStruct((MATS, ROWS, COLS), jnp.bfloat16),
        ],
        compiler_params=params(),
        cost_estimate=pl.CostEstimate(
            flops=500_000_000, bytes_accessed=7_000_000, transcendentals=0
        ),
        name="outputs",
    )(place, small, top, rest, ortho, residual, weight)


ROW_AXES = ("zh", "zl", "yh", "yl")


def shift(value, z_step, y_step):
    pairs = [
        (z * 8 + y, (z + z_step) % 8 * 8 + (y + y_step) % 8) for z in range(8) for y in range(8)
    ]
    return lax.ppermute(value, ROW_AXES, pairs)


def swap(value, z_flip, y_flip):
    pairs = [(z * 8 + y, (z ^ z_flip) * 8 + (y ^ y_flip)) for z in range(8) for y in range(8)]
    return lax.ppermute(value, ROW_AXES, pairs)


def per_device(codes, scales, table, gradient, weight, basis):
    place = jnp.stack([lax.axis_index(axis) for axis in ("yl", "x", "zl", "core")])
    place = place.astype(jnp.int32)
    tables = jnp.concatenate(
        [jnp.swapaxes(scales, 1, 2).reshape(8, ROWS), table.reshape(2, 128)], axis=0
    )
    *blocks, partial_power = decode(place, codes, tables, gradient, basis)

    from_y = swap(blocks[1], 0, 1)
    from_z = swap(blocks[2], 1, 0)
    from_diagonal = swap(blocks[3], 1, 1)

    pieces = lax.all_to_all(partial_power.reshape(8, 32, RANK), COLS_AXES, 0, 0, tiled=True)
    piece = jnp.sum(pieces, axis=0)
    near = everyone(piece, GROUP)
    far = lax.ppermute(near, "core", [(0, 1), (1, 0)])

    near_rows = stack_rows(blocks[0], from_y)
    far_rows = stack_rows(from_z, from_diagonal)
    pieces, power = cross(place, (*near_rows, *far_rows), near, far)
    pieces = lax.all_to_all(pieces, OTHERS, 0, 0, tiled=True)
    piece = jnp.sum(pieces, axis=0)
    own = everyone(piece, OTHERS)
    plain, gram = part(own)
    y = shift(plain, 0, 1)
    z = shift(plain, 1, 0)
    diagonal = shift(plain, -1, -1)
    gram = lax.all_to_all(gram, COLS_AXES, 0, 0, tiled=True)
    inv = inverse_factor(gram)

    top, rest, ortho, residual, small = finish(place, inv, power, (plain, y, z, diagonal), blocks)
    small = everyone(small, COLS_AXES)
    new_momentum, peaks, new_basis, new_weight = outputs(
        place, small, top, rest, ortho, residual, weight
    )
    return new_momentum, jnp.swapaxes(peaks, 1, 2), new_basis, new_weight


def solution(mesh):
    axes = ("zh", "zl", "yh", "yl", "x", "core")
    fine = Mesh(mesh.devices.reshape(4, 2, 4, 2, 4, 2), axes)
    rows = axes[:4]
    cols = axes[4:]
    return jax.shard_map(
        per_device,
        mesh=fine,
        in_specs=(
            P(None, rows, cols),
            P(None, rows, None),
            P(),
            P(None, rows, cols),
            P(None, rows, cols),
            P(None, cols, None),
        ),
        out_specs=(
            P(None, rows, cols),
            P(None, rows, None),
            P(None, cols, None),
            P(None, rows, cols),
        ),
        check_vma=False,
    )
```
